128 devices in a mesh: seq: 4 (over x), expert: 32 (over z, y, core).
Axes of the slice: x: 4, y: 4, z: 4, core: 2. Of those that a mesh axis runs over, the one named last changes fastest.
Arguments:
- tokens: bfloat16 [32, 1024, 4096], P('expert', 'seq'), may hold values from -6 to 6
- norm_gain: float32 [4096], replicated, may hold values from 0.1 to 1.9
- conv_weight: float32 [4, 4096], replicated, may hold values from -3 to 3
- conv_bias: float32 [4096], replicated, may hold values from -3 to 3
- proj_weight: bfloat16 [4096, 288], replicated, may hold values from -0.09375 to 0.09375
- dt_weight: bfloat16 [256, 4096], replicated, may hold values from -0.375 to 0.375
- dt_bias: float32 [4096], replicated, may hold values from -4 to 0
- decay_rate: float32 [16, 4096], replicated, may hold values from 0.02 to 1
- skip_gain: float32 [4096], replicated, may hold values from 0.5 to 1.5
- ffn_gain: float32 [4096], replicated, may hold values from 0.1 to 1.9
- expert_ids: int32 [32, 1024, 2], P('expert', 'seq'), may hold values from 0 to 31, all different within a row; in each aligned block of 256 rows (0 to 255, 256 to 511, ..., all dimensions but the last counted through in order) at most 32 rows name the same one
- route_weights: float32 [32, 1024, 2], P('expert', 'seq'), may hold values from 0.2 to 1
- w_gate: bfloat16 [32, 4096, 512], P('expert'), may hold values from -0.09375 to 0.09375
- w_up: bfloat16 [32, 4096, 512], P('expert'), may hold values from -0.09375 to 0.09375
- w_down: bfloat16 [32, 512, 4096], P('expert'), may hold values from -0.25 to 0.25
Outputs:
- block_out: bfloat16 [32, 1024, 4096], P('expert', 'seq')
The draws below stay inside these ranges and needn't reach their ends.
Inputs may be any that keep to these rules, and one draw needn't show every extreme that they name: `expert_ids`: the two expert slices of a position differ. Among the 256 positions of one device, no expert slice is chosen more than 32 times, and in every draw some expert slice is chosen exactly 32 times by the positions of some device; every expert slice is chosen somewhere.
All inputs are finite; a program needn't handle non-finite values.
Results may differ from the reference program's by a relative error of at most 0.0085.
Values may be sent and summed in bfloat16 or wider, within the bound.
A program may use at most 128 MiB of HBM per device.

```python
import math
import jax
import jax.numpy as jnp
import numpy as np
from jax import lax

D = 4096
FF = 512
STATE = 16
DT_RANK = 256
CONV = 4
TOK_DEV = 256
LEN = 1024
BATCH = 32
EXPERTS = 32
CAP = 32
N_SEQ = 4


def levels(key, dims, shards, least, high):
    def one(position, blocks):
        heights = jax.random.uniform(jax.random.fold_in(jax.random.fold_in(key, 6), position), (blocks,), jnp.float32, least / len(shards), high / len(shards))
        return jnp.repeat(jnp.exp(heights), dims[position] // blocks).reshape((-1,) + (1,) * (len(dims) - position - 1))

    level = one(*shards[0])
    for cut in shards[1:]:
        level = level * one(*cut)
    return level


def assign_block(stream_key, own, number, rows, count, top, reach, lean):
    ranking = jax.random.permutation(stream_key, count)
    heavy_load, common = load_shares(count, rows * top, reach, lean, True), load_shares(count, rows * top, reach, lean, False)
    places = jnp.arange(count)

    def named(tallies, turn):
        used = int((tallies > 0).sum())
        fixed = max(1, used // 4)
        shifted = fixed + (places - fixed + turn * (used - fixed)) % max(1, count - fixed)
        return jnp.zeros((count,), jnp.int32).at[ranking[jnp.where(places < fixed, places, shifted)]].set(jnp.asarray(tallies, jnp.int32))

    tallies = jnp.where(number % 4 == 0, named(heavy_load, number // 4), named(common, number - number // 4 - 1))
    mixed = jax.random.permutation(jax.random.fold_in(own, 3), count)
    donor, sink = mixed[0:count // 2 * 2:2], mixed[1:count // 2 * 2:2]
    margin = jnp.minimum(tallies[donor] - 1, reach - tallies[sink]) // 2
    margin = jnp.where((donor == ranking[0]) | (sink == ranking[0]) | (tallies[sink] == 0), 0, jnp.maximum(margin, 0))
    shifted = jax.random.randint(jax.random.fold_in(own, 4), (count // 2,), 0, 1 << 20) % (margin + 1)
    tallies = tallies.at[donor].add(-shifted).at[sink].add(shifted)
    members = jnp.searchsorted(jnp.cumsum(tallies), jnp.arange(rows * top), side="right").astype(jnp.int32)
    listing = members.reshape(top, rows).T
    listing = listing[jax.random.permutation(jax.random.fold_in(own, 1), rows)]
    turn = jax.random.randint(jax.random.fold_in(own, 2), (rows, 1), 0, top)
    return jnp.take_along_axis(listing, (jnp.arange(top)[None, :] + turn) % top, axis=1)


def load_shares(count, total, most, slope, full):
    weights = [(1 << 20) // math.isqrt(rank ** slope) + 1 for rank in range(1, count + 1)]
    largest = most if full else min(most, max(-(-total // count), total * weights[0] // sum(weights)))
    least = 1 if total - largest >= count - 1 else 0
    holding, rest = [largest] + [least] * (count - 1), total - largest - least * (count - 1)
    while rest > 0:
        free = [i for i in range(1, count) if holding[i] < largest] or [i for i in range(1, count) if holding[i] < most]
        mass, budget = sum([weights[i] for i in free]), rest
        for i in free:
            extra = min(most - holding[i], max(1, budget * weights[i] // mass), rest)
            holding[i] = holding[i] + extra
            rest = rest - extra
    return np.array(holding)


def normal_values(stream_key, dims, deviation, reach, shards=(), kind=jnp.bfloat16):
    values = deviation * jax.random.normal(stream_key, dims, jnp.float32)
    if shards:
        values = values * levels(stream_key, dims, shards, -0.22, 0.18)
    return jnp.clip(values, -reach, reach).astype(kind)


def setup_inputs(seed: int = 0) -> dict:
    key_list = jax.random.split(jax.random.key(seed), 16)
    tokens = normal_values(key_list[0], (BATCH, LEN, D), 1.0, 6.0, ((0, 32), (1, 4)))
    norm_gain = jnp.clip(1.0 + 0.18 * jax.random.normal(key_list[1], (D,), jnp.float32), 0.1, 1.9)
    conv_weight = normal_values(key_list[2], (CONV, D), CONV ** -0.5, 3.0, (), jnp.float32)
    conv_bias = normal_values(key_list[3], (D,), 0.5, 3.0, (), jnp.float32)
    proj_weight = normal_values(key_list[4], (D, DT_RANK + 2 * STATE), D ** -0.5, 0.09375)
    dt_weight = normal_values(key_list[5], (DT_RANK, D), DT_RANK ** -0.5, 0.375)
    dt_bias = jnp.clip(jax.random.uniform(key_list[6], (D,), jnp.float32, -4.0, 0.0), -4.0, 0.0)
    decay_rate = jnp.clip(jnp.exp(jax.random.uniform(key_list[7], (STATE, D), jnp.float32, math.log(0.02), math.log(1.0))), 0.02, 1.0)
    skip_gain = jnp.clip(jax.random.uniform(key_list[8], (D,), jnp.float32, 0.5, 1.5), 0.5, 1.5)
    ffn_gain = jnp.clip(1.0 + 0.18 * jax.random.normal(key_list[9], (D,), jnp.float32), 0.1, 1.9)
    expert_ids_keys = jax.random.split(jax.random.fold_in(key_list[10], 1), BATCH * LEN // TOK_DEV)
    expert_ids_turns = jax.random.permutation(jax.random.fold_in(key_list[10], 3), BATCH * LEN // TOK_DEV)
    expert_ids = jax.vmap(lambda own, number: assign_block(jax.random.fold_in(key_list[10], 2), own, number, TOK_DEV, EXPERTS, 2, CAP, 2))(expert_ids_keys, expert_ids_turns).reshape((BATCH, LEN, 2))
    route_weights = jnp.clip(0.2 + 0.8 * jax.random.uniform(key_list[11], (BATCH, LEN, 2), jnp.float32) ** levels(key_list[11], (BATCH, LEN, 2), ((0, 32), (1, 4)), -0.2, 0.2), 0.2, 1.0)
    w_gate = normal_values(key_list[12], (EXPERTS, D, FF), D ** -0.5, 0.09375, ((0, 32),))
    w_up = normal_values(key_list[13], (EXPERTS, D, FF), D ** -0.5, 0.09375, ((0, 32),))
    w_down = normal_values(key_list[14], (EXPERTS, FF, D), FF ** -0.5, 0.25, ((0, 32),))
    return {"tokens": tokens, "norm_gain": norm_gain, "conv_weight": conv_weight, "conv_bias": conv_bias, "proj_weight": proj_weight, "dt_weight": dt_weight, "dt_bias": dt_bias, "decay_rate": decay_rate, "skip_gain": skip_gain, "ffn_gain": ffn_gain, "expert_ids": expert_ids, "route_weights": route_weights, "w_gate": w_gate, "w_up": w_up, "w_down": w_down}


def rms_scale(values, gain):
    return values * lax.rsqrt(lax.optimization_barrier(jnp.mean(values * values, axis=-1, keepdims=True)) + 1e-05) * gain

def reference(tokens, norm_gain, conv_weight, conv_bias, proj_weight, dt_weight, dt_bias, decay_rate, skip_gain, ffn_gain, expert_ids, route_weights, w_gate, w_up, w_down):
    stream = tokens.astype(jnp.float32)
    normed = rms_scale(stream, norm_gain).astype(jnp.bfloat16)
    padded = jnp.pad(normed.astype(jnp.float32), ((0, 0), (CONV - 1, 0), (0, 0)))
    conv_sum = jnp.zeros((BATCH, LEN, D), jnp.float32)
    for offset in range(CONV):
        conv_sum = conv_sum + conv_weight[offset] * padded[:, offset:offset + LEN]
    conv_out = jax.nn.silu(conv_sum + conv_bias).astype(jnp.bfloat16)
    conv_rows = conv_out.reshape(BATCH * LEN, D)
    projected = jnp.dot(conv_rows, proj_weight, preferred_element_type=jnp.float32)
    low_rank = projected[:, :DT_RANK].astype(jnp.bfloat16)
    step_size = jax.nn.softplus(jnp.dot(low_rank, dt_weight, preferred_element_type=jnp.float32) + dt_bias)
    input_map = projected[:, DT_RANK:DT_RANK + STATE]
    output_map = projected[:, DT_RANK + STATE:]
    decay_neg = -decay_rate
    conv_float = conv_out.astype(jnp.float32)
    step_time = step_size.reshape(BATCH, LEN, D).transpose(1, 0, 2)
    conv_time = conv_float.transpose(1, 0, 2)
    input_time = input_map.reshape(BATCH, LEN, STATE).transpose(1, 0, 2)
    output_time = output_map.reshape(BATCH, LEN, STATE).transpose(1, 0, 2)

    def advance(ssm_state, pieces):
        step_now, input_now, in_now, out_now = pieces
        ssm_state = jnp.exp(step_now[:, None, :] * decay_neg) * ssm_state + (step_now * input_now)[:, None, :] * in_now[:, :, None]
        return (ssm_state, lax.optimization_barrier(jnp.sum(out_now[:, :, None] * ssm_state, axis=1)))
    _, collected = lax.scan(advance, jnp.zeros((BATCH, STATE, D), jnp.float32), (step_time, conv_time, input_time, output_time))
    scanned = collected.transpose(1, 0, 2)
    hidden_state = stream + (scanned + skip_gain * conv_float)
    ffn_in = rms_scale(hidden_state, ffn_gain).astype(jnp.bfloat16).reshape(BATCH * LEN, D)
    blocks = BATCH * N_SEQ
    pair_count = 2 * TOK_DEV
    chosen = expert_ids.reshape(blocks, pair_count).astype(jnp.int32)
    onehot = (chosen[:, :, None] == jnp.arange(EXPERTS, dtype=jnp.int32)[None, None, :]).astype(jnp.int32)
    before = jnp.cumsum(onehot, axis=1) - onehot
    slot_pos = lax.optimization_barrier(jnp.sum(before * onehot, axis=2)).astype(jnp.int32)
    block_index = jnp.broadcast_to(jnp.arange(blocks, dtype=jnp.int32)[:, None], (blocks, pair_count))
    assign = jnp.arange(blocks * pair_count, dtype=jnp.int32).reshape(blocks, pair_count)
    slot_table = jnp.full((EXPERTS, blocks, CAP), -1, jnp.int32).at[chosen, block_index, slot_pos].set(assign)
    weights_flat = route_weights.reshape(-1)

    def expert_pass(routed, pieces):
        rows_index, gate_mat, up_mat, down_mat = pieces
        rows_index = rows_index.reshape(-1)
        usable = rows_index >= 0
        clipped = jnp.where(usable, rows_index, 0).astype(jnp.int32)
        token_index = (clipped // 2).astype(jnp.int32)
        rows_in = jnp.where(usable[:, None], ffn_in[token_index], jnp.zeros((), ffn_in.dtype))
        gate_part = jnp.dot(rows_in, gate_mat, preferred_element_type=jnp.float32)
        up_part = jnp.dot(rows_in, up_mat, preferred_element_type=jnp.float32)
        inner_act = (jax.nn.silu(gate_part) * up_part).astype(jnp.bfloat16)
        result = jnp.dot(inner_act, down_mat, preferred_element_type=jnp.float32).astype(jnp.bfloat16).astype(jnp.float32)
        route_scale = jnp.where(usable, weights_flat[clipped], jnp.zeros((), weights_flat.dtype))
        return (routed.at[token_index].add(route_scale[:, None] * result), None)
    routed, _ = lax.scan(expert_pass, jnp.zeros((BATCH * LEN, D), jnp.float32), (slot_table, w_gate, w_up, w_down))
    block_out = (hidden_state.reshape(BATCH * LEN, D) + routed).astype(jnp.bfloat16)
    return block_out.reshape(BATCH, LEN, D)
```

```python
import jax
import jax.numpy as jnp
from jax import lax
from jax.sharding import PartitionSpec as P
from jax.experimental import pallas as pl
from jax.experimental.pallas import tpu as pltpu


def from_behind(array, axis, by):
    peers = lax.axis_size(axis)
    pairs = [(i, i + by) for i in range(peers) if 0 <= i + by < peers]
    return lax.ppermute(array, axis, pairs)


def prefix(array, axis, combine, identity):
    peers, place = (lax.axis_size(axis), lax.axis_index(axis))
    everything = jax.tree.map(lambda part: lax.all_gather(part, axis), array)
    start = jax.tree.map(
        lambda part, zero: jnp.broadcast_to(jnp.asarray(zero, part.dtype), part.shape),
        array,
        identity,
    )

    def turn(k, before):
        reached = k < place
        new = combine(before, jax.tree.map(lambda part: part[k], everything))
        return jax.tree.map(lambda a, b: jnp.where(reached, a, b), new, before)

    return lax.fori_loop(0, peers, turn, start)


def rms_scale(values, gain):
    return values * lax.rsqrt(jnp.mean(values * values, axis=-1, keepdims=True) + 1e-05) * gain


def scan_kernel(with_output):
    def body(in_ref, out_ref, step_ref, drive_ref, decay_ref, init_ref, *outs):
        states = decay_ref.shape[0]
        tok_count = step_ref.shape[0]
        decay_rows = [decay_ref[n] for n in range(states)]
        if with_output:
            y_ref, end_ref = outs
        else:
            (end_ref,) = outs

        def turn(t, carry):
            step_now = step_ref[t]
            drive_now = drive_ref[t]
            base = t * states
            total = None
            fresh = []
            for n in range(states):
                value = jnp.exp(step_now * decay_rows[n]) * carry[n] + drive_now * in_ref[base + n]
                fresh.append(value)
                if with_output:
                    part = out_ref[base + n] * value
                    total = part if total is None else total + part
            if with_output:
                y_ref[t] = total
            return tuple(fresh)

        start = tuple(init_ref[n] for n in range(states))
        final = lax.fori_loop(0, tok_count, turn, start, unroll=2)
        for n in range(states):
            end_ref[n] = final[n]

    return body


def local_scan(start_state, step_size, drive, input_map, output_map, decay_neg, with_output):
    tok_count, model_width = step_size.shape
    states = decay_neg.shape[0]
    lanes = 128
    rows = model_width // lanes
    blk = 8
    step3 = step_size.reshape(tok_count, rows, lanes)
    drive3 = drive.reshape(tok_count, rows, lanes)
    decay3 = decay_neg.reshape(states, rows, lanes)
    init3 = start_state.reshape(states, rows, lanes)
    smem = pl.BlockSpec(memory_space=pltpu.SMEM)
    seq_spec = pl.BlockSpec((tok_count, blk, lanes), lambda j: (0, j, 0))
    st_spec = pl.BlockSpec((states, blk, lanes), lambda j: (0, j, 0))
    out_shape = [jax.ShapeDtypeStruct((states, rows, lanes), jnp.float32)]
    out_specs = [st_spec]
    if with_output:
        out_shape.insert(0, jax.ShapeDtypeStruct((tok_count, rows, lanes), jnp.float32))
        out_specs.insert(0, seq_spec)
    results = pl.pallas_call(
        scan_kernel(with_output),
        grid=(rows // blk,),
        in_specs=[smem, smem, seq_spec, seq_spec, st_spec, st_spec],
        out_specs=out_specs,
        out_shape=out_shape,
    )(input_map.reshape(-1), output_map.reshape(-1), step3, drive3, decay3, init3)
    end_state = results[-1].reshape(states, model_width)
    if with_output:
        return (results[0].reshape(tok_count, model_width), end_state)
    return (None, end_state)


def per_device(
    tokens,
    norm_gain,
    conv_weight,
    conv_bias,
    proj_weight,
    dt_weight,
    dt_bias,
    decay_rate,
    skip_gain,
    ffn_gain,
    expert_ids,
    route_weights,
    w_gate,
    w_up,
    w_down,
):
    stream = tokens[0].astype(jnp.float32)
    tok_count = stream.shape[0]
    model_width = stream.shape[1]
    kernel = conv_weight.shape[0]
    low_width = dt_weight.shape[0]
    states = decay_rate.shape[0]
    normed = rms_scale(stream, norm_gain).astype(jnp.bfloat16)
    prior_rows = from_behind(normed[tok_count - (kernel - 1) :], "seq", 1)
    padded = jnp.concatenate([prior_rows, normed], axis=0).astype(jnp.float32)
    conv_sum = jnp.zeros((tok_count, model_width), jnp.float32)
    for offset in range(kernel):
        conv_sum = conv_sum + conv_weight[offset] * padded[offset : offset + tok_count]
    conv_out = jax.nn.silu(conv_sum + conv_bias).astype(jnp.bfloat16)
    projected = jnp.dot(conv_out, proj_weight, preferred_element_type=jnp.float32)
    low_rank = projected[:, :low_width].astype(jnp.bfloat16)
    step_size = jax.nn.softplus(
        jnp.dot(low_rank, dt_weight, preferred_element_type=jnp.float32) + dt_bias
    )
    input_map = projected[:, low_width : low_width + states]
    output_map = projected[:, low_width + states :]
    decay_neg = -decay_rate
    conv_float = conv_out.astype(jnp.float32)
    zero_state = jnp.zeros((states, model_width), jnp.float32)
    drive = step_size * conv_float
    _, end_state = local_scan(
        zero_state, step_size, drive, input_map, output_map, decay_neg, False
    )
    span_decay = jnp.exp(decay_neg * jnp.sum(step_size, axis=0)[None, :])

    def compose(earlier, latter):
        return (earlier[0] * latter[0], latter[0] * earlier[1] + latter[1])

    peers, place = (lax.axis_size("seq"), lax.axis_index("seq"))
    everything = lax.all_gather(jnp.stack([span_decay, end_state]), "seq")
    incoming = jnp.zeros_like(end_state)
    for k in range(peers):
        moved = everything[k, 0] * incoming + everything[k, 1]
        incoming = jnp.where(k < place, moved, incoming)
    scanned, _ = local_scan(incoming, step_size, drive, input_map, output_map, decay_neg, True)
    hidden_state = stream + (scanned + skip_gain * conv_float)
    ffn_in = rms_scale(hidden_state, ffn_gain).astype(jnp.bfloat16)
    owners = lax.axis_size("expert")
    experts = owners * w_gate.shape[0]
    capacity = 4 * tok_count // owners
    chosen = expert_ids[0].reshape(-1)
    onehot = (chosen[:, None] == jnp.arange(experts, dtype=jnp.int32)[None, :]).astype(jnp.int32)
    before = jnp.cumsum(onehot, axis=0) - onehot
    slot_pos = jnp.sum(before * onehot, axis=1)
    dest_row = chosen * capacity + slot_pos
    outgoing = (
        jnp.zeros((experts * capacity, model_width), jnp.bfloat16)
        .at[dest_row]
        .set(jnp.repeat(ffn_in, 2, axis=0))
    )
    outgoing = outgoing.reshape(experts, capacity, model_width)
    received = lax.all_to_all(outgoing, "expert", split_axis=0, concat_axis=0, tiled=True)
    recv_shape = received.shape
    rows_in = received.reshape(-1, model_width)
    gate_part = jnp.dot(rows_in, w_gate[0], preferred_element_type=jnp.float32)
    up_part = jnp.dot(rows_in, w_up[0], preferred_element_type=jnp.float32)
    inner_act = (jax.nn.silu(gate_part) * up_part).astype(jnp.bfloat16)
    result = jnp.dot(inner_act, w_down[0], preferred_element_type=jnp.float32).astype(jnp.bfloat16)
    returned = lax.all_to_all(
        result.reshape(recv_shape), "expert", split_axis=0, concat_axis=0, tiled=True
    )
    gathered = returned.reshape(experts * capacity, model_width)[dest_row].astype(jnp.float32)
    route_scale = route_weights[0].reshape(-1)
    weighted = (route_scale[:, None] * gathered).reshape(tok_count, 2, model_width)
    routed = weighted[:, 0] + weighted[:, 1]
    block_out = (hidden_state + routed).astype(jnp.bfloat16)
    return block_out[None]


def solution(mesh):
    in_specs = (
        P("expert", "seq", None),
        P(),
        P(),
        P(),
        P(),
        P(),
        P(),
        P(),
        P(),
        P(),
        P("expert", "seq", None),
        P("expert", "seq", None),
        P("expert", None, None),
        P("expert", None, None),
        P("expert", None, None),
    )
    out_specs = P("expert", "seq", None)
    return jax.shard_map(
        per_device, mesh=mesh, in_specs=in_specs, out_specs=out_specs, check_vma=False
    )
```

```python
import jax
import jax.numpy as jnp
from jax import lax
from jax.sharding import PartitionSpec as P
from jax.experimental import pallas as pl
from jax.experimental.pallas import tpu as pltpu


def from_behind(array, axis, by):
    peers = lax.axis_size(axis)
    pairs = [(i, i + by) for i in range(peers) if 0 <= i + by < peers]
    return lax.ppermute(array, axis, pairs)


def prefix(array, axis, combine, identity):
    peers, place = (lax.axis_size(axis), lax.axis_index(axis))
    everything = jax.tree.map(lambda part: lax.all_gather(part, axis), array)
    start = jax.tree.map(
        lambda part, zero: jnp.broadcast_to(jnp.asarray(zero, part.dtype), part.shape),
        array,
        identity,
    )

    def turn(k, before):
        reached = k < place
        new = combine(before, jax.tree.map(lambda part: part[k], everything))
        return jax.tree.map(lambda a, b: jnp.where(reached, a, b), new, before)

    return lax.fori_loop(0, peers, turn, start)


def rms_scale(values, gain):
    return values * lax.rsqrt(jnp.mean(values * values, axis=-1, keepdims=True) + 1e-05) * gain


def scan_kernel(with_output):
    def body(in_ref, out_ref, step_ref, drive_ref, decay_ref, init_ref, *outs):
        states = decay_ref.shape[0]
        tok_count = step_ref.shape[0]
        decay_rows = [decay_ref[n] for n in range(states)]
        if with_output:
            y_ref, end_ref = outs
        else:
            (end_ref,) = outs

        def turn(t, carry):
            step_now = step_ref[t]
            drive_now = drive_ref[t]
            base = t * states
            total = None
            fresh = []
            for n in range(states):
                value = jnp.exp(step_now * decay_rows[n]) * carry[n] + drive_now * in_ref[base + n]
                fresh.append(value)
                if with_output:
                    part = out_ref[base + n] * value
                    total = part if total is None else total + part
            if with_output:
                y_ref[t] = total
            return tuple(fresh)

        start = tuple(init_ref[n] for n in range(states))
        final = lax.fori_loop(0, tok_count, turn, start, unroll=2)
        for n in range(states):
            end_ref[n] = final[n]

    return body


def local_scan(start_state, step_size, drive, input_map, output_map, decay_neg, with_output):
    tok_count, model_width = step_size.shape
    states = decay_neg.shape[0]
    lanes = 128
    rows = model_width // lanes
    blk = 8
    step3 = step_size.reshape(tok_count, rows, lanes)
    drive3 = drive.reshape(tok_count, rows, lanes)
    decay3 = decay_neg.reshape(states, rows, lanes)
    init3 = start_state.reshape(states, rows, lanes)
    smem = pl.BlockSpec(memory_space=pltpu.SMEM)
    seq_spec = pl.BlockSpec((tok_count, blk, lanes), lambda j: (0, j, 0))
    st_spec = pl.BlockSpec((states, blk, lanes), lambda j: (0, j, 0))
    out_shape = [jax.ShapeDtypeStruct((states, rows, lanes), jnp.float32)]
    out_specs = [st_spec]
    if with_output:
        out_shape.insert(0, jax.ShapeDtypeStruct((tok_count, rows, lanes), jnp.float32))
        out_specs.insert(0, seq_spec)
    results = pl.pallas_call(
        scan_kernel(with_output),
        grid=(rows // blk,),
        in_specs=[smem, smem, seq_spec, seq_spec, st_spec, st_spec],
        out_specs=out_specs,
        out_shape=out_shape,
    )(input_map.reshape(-1), output_map.reshape(-1), step3, drive3, decay3, init3)
    end_state = results[-1].reshape(states, model_width)
    if with_output:
        return (results[0].reshape(tok_count, model_width), end_state)
    return (None, end_state)


def per_device(
    tokens,
    norm_gain,
    conv_weight,
    conv_bias,
    proj_weight,
    dt_weight,
    dt_bias,
    decay_rate,
    skip_gain,
    ffn_gain,
    expert_ids,
    route_weights,
    w_gate,
    w_up,
    w_down,
):
    stream = tokens[0].astype(jnp.float32)
    tok_count = stream.shape[0]
    model_width = stream.shape[1]
    kernel = conv_weight.shape[0]
    low_width = dt_weight.shape[0]
    states = decay_rate.shape[0]
    normed = rms_scale(stream, norm_gain).astype(jnp.bfloat16)
    prior_rows = from_behind(normed[tok_count - (kernel - 1) :], "seq", 1)
    padded = jnp.concatenate([prior_rows, normed], axis=0).astype(jnp.float32)
    conv_sum = jnp.zeros((tok_count, model_width), jnp.float32)
    for offset in range(kernel):
        conv_sum = conv_sum + conv_weight[offset] * padded[offset : offset + tok_count]
    conv_out = jax.nn.silu(conv_sum + conv_bias).astype(jnp.bfloat16)
    projected = jnp.dot(conv_out, proj_weight, preferred_element_type=jnp.float32)
    low_rank = projected[:, :low_width].astype(jnp.bfloat16)
    step_size = jax.nn.softplus(
        jnp.dot(low_rank, dt_weight, preferred_element_type=jnp.float32) + dt_bias
    )
    input_map = projected[:, low_width : low_width + states]
    output_map = projected[:, low_width + states :]
    decay_neg = -decay_rate
    conv_float = conv_out.astype(jnp.float32)
    zero_state = jnp.zeros((states, model_width), jnp.float32)
    drive = step_size * conv_float
    _, end_state = local_scan(
        zero_state, step_size, drive, input_map, output_map, decay_neg, False
    )
    span_decay = jnp.exp(decay_neg * jnp.sum(step_size, axis=0)[None, :])

    def compose(earlier, latter):
        return (earlier[0] * latter[0], latter[0] * earlier[1] + latter[1])

    peers = lax.axis_size("seq")
    summary = jnp.stack([span_decay, end_state])
    arrived = [from_behind(summary, "seq", k) for k in range(peers - 1, 0, -1)]
    incoming = jnp.zeros_like(end_state)
    for piece in arrived:
        incoming = piece[0] * incoming + piece[1]
    scanned, _ = local_scan(incoming, step_size, drive, input_map, output_map, decay_neg, True)
    hidden_state = stream + (scanned + skip_gain * conv_float)
    ffn_in = rms_scale(hidden_state, ffn_gain).astype(jnp.bfloat16)
    owners = lax.axis_size("expert")
    experts = owners * w_gate.shape[0]
    capacity = 4 * tok_count // owners
    chosen = expert_ids[0].reshape(-1)
    onehot = (chosen[:, None] == jnp.arange(experts, dtype=jnp.int32)[None, :]).astype(jnp.int32)
    before = jnp.cumsum(onehot, axis=0) - onehot
    slot_pos = jnp.sum(before * onehot, axis=1)
    dest_row = chosen * capacity + slot_pos
    slot_ids = jnp.arange(experts * capacity, dtype=jnp.int32)
    pair_rows = dest_row.reshape(tok_count, 2)
    place_map = (
        (slot_ids[:, None] == pair_rows[None, :, 0]) | (slot_ids[:, None] == pair_rows[None, :, 1])
    ).astype(jnp.bfloat16)
    outgoing = jnp.dot(place_map, ffn_in, preferred_element_type=jnp.float32).astype(jnp.bfloat16)
    outgoing = outgoing.reshape(experts, capacity, model_width)
    received = lax.all_to_all(outgoing, "expert", split_axis=0, concat_axis=0, tiled=True)
    recv_shape = received.shape
    rows_in = received.reshape(-1, model_width)
    gate_part = jnp.dot(rows_in, w_gate[0], preferred_element_type=jnp.float32)
    up_part = jnp.dot(rows_in, w_up[0], preferred_element_type=jnp.float32)
    inner_act = (jax.nn.silu(gate_part) * up_part).astype(jnp.bfloat16)
    result = jnp.dot(inner_act, w_down[0], preferred_element_type=jnp.float32).astype(jnp.bfloat16)
    returned = lax.all_to_all(
        result.reshape(recv_shape), "expert", split_axis=0, concat_axis=0, tiled=True
    )
    flat_back = returned.reshape(experts * capacity, model_width)
    picks = [
        jnp.dot(
            (pair_rows[:, k][:, None] == slot_ids[None, :]).astype(jnp.bfloat16),
            flat_back,
            preferred_element_type=jnp.float32,
        )
        for k in range(2)
    ]
    route_scale = route_weights[0]
    routed = route_scale[:, 0:1] * picks[0] + route_scale[:, 1:2] * picks[1]
    block_out = (hidden_state + routed).astype(jnp.bfloat16)
    return block_out[None]


def solution(mesh):
    in_specs = (
        P("expert", "seq", None),
        P(),
        P(),
        P(),
        P(),
        P(),
        P(),
        P(),
        P(),
        P(),
        P("expert", "seq", None),
        P("expert", "seq", None),
        P("expert", None, None),
        P("expert", None, None),
        P("expert", None, None),
    )
    out_specs = P("expert", "seq", None)
    return jax.shard_map(
        per_device, mesh=mesh, in_specs=in_specs, out_specs=out_specs, check_vma=False
    )
```

```python
import jax
import jax.numpy as jnp
from jax import lax
from jax.sharding import PartitionSpec as P
from jax.experimental import pallas as pl
from jax.experimental.pallas import tpu as pltpu


def from_behind(array, axis, by):
    peers = lax.axis_size(axis)
    pairs = [(i, i + by) for i in range(peers) if 0 <= i + by < peers]
    return lax.ppermute(array, axis, pairs)


def prefix(array, axis, combine, identity):
    peers, place = (lax.axis_size(axis), lax.axis_index(axis))
    everything = jax.tree.map(lambda part: lax.all_gather(part, axis), array)
    start = jax.tree.map(
        lambda part, zero: jnp.broadcast_to(jnp.asarray(zero, part.dtype), part.shape),
        array,
        identity,
    )

    def turn(k, before):
        reached = k < place
        new = combine(before, jax.tree.map(lambda part: part[k], everything))
        return jax.tree.map(lambda a, b: jnp.where(reached, a, b), new, before)

    return lax.fori_loop(0, peers, turn, start)


def rms_scale(values, gain):
    return values * lax.rsqrt(jnp.mean(values * values, axis=-1, keepdims=True) + 1e-05) * gain


def scan_kernel(with_output):
    def body(in_ref, out_ref, step_ref, drive_ref, decay_ref, init_ref, *outs):
        states = decay_ref.shape[0]
        tok_count = step_ref.shape[0]
        decay_rows = [decay_ref[n] for n in range(states)]
        if with_output:
            y_ref, end_ref = outs
        else:
            (end_ref,) = outs

        def turn(t, carry):
            step_now = step_ref[t]
            drive_now = drive_ref[t]
            base = t * states
            total = None
            fresh = []
            for n in range(states):
                value = jnp.exp(step_now * decay_rows[n]) * carry[n] + drive_now * in_ref[base + n]
                fresh.append(value)
                if with_output:
                    part = out_ref[base + n] * value
                    total = part if total is None else total + part
            if with_output:
                y_ref[t] = total
            return tuple(fresh)

        start = tuple(init_ref[n] for n in range(states))
        final = lax.fori_loop(0, tok_count, turn, start, unroll=2)
        for n in range(states):
            end_ref[n] = final[n]

    return body


def local_scan(start_state, step3, drive3, input_map, output_map, decay3, with_output, first, count):
    tok_count, rows, lanes = step3.shape
    states = decay3.shape[0]
    blk = 8
    grid_len = count // blk
    lead = first // blk
    smem = pl.BlockSpec(memory_space=pltpu.SMEM)
    seq_spec = pl.BlockSpec((tok_count, blk, lanes), lambda j: (0, j + lead, 0))
    st_spec = pl.BlockSpec((states, blk, lanes), lambda j: (0, j + lead, 0))
    own_seq = pl.BlockSpec((tok_count, blk, lanes), lambda j: (0, j, 0))
    own_st = pl.BlockSpec((states, blk, lanes), lambda j: (0, j, 0))
    out_shape = [jax.ShapeDtypeStruct((states, count, lanes), jnp.float32)]
    out_specs = [own_st]
    if with_output:
        out_shape.insert(0, jax.ShapeDtypeStruct((tok_count, count, lanes), jnp.float32))
        out_specs.insert(0, own_seq)
    results = pl.pallas_call(
        scan_kernel(with_output),
        grid=(grid_len,),
        in_specs=[smem, smem, seq_spec, seq_spec, st_spec, own_st],
        out_specs=out_specs,
        out_shape=out_shape,
    )(input_map.reshape(-1), output_map.reshape(-1), step3, drive3, decay3, start_state)
    if with_output:
        return (results[0], results[-1])
    return (None, results[-1])


def per_device(
    tokens,
    norm_gain,
    conv_weight,
    conv_bias,
    proj_weight,
    dt_weight,
    dt_bias,
    decay_rate,
    skip_gain,
    ffn_gain,
    expert_ids,
    route_weights,
    w_gate,
    w_up,
    w_down,
):
    stream = tokens[0].astype(jnp.float32)
    tok_count = stream.shape[0]
    model_width = stream.shape[1]
    kernel = conv_weight.shape[0]
    low_width = dt_weight.shape[0]
    states = decay_rate.shape[0]
    normed = rms_scale(stream, norm_gain).astype(jnp.bfloat16)
    prior_rows = from_behind(normed[tok_count - (kernel - 1) :], "seq", 1)
    padded = jnp.concatenate([prior_rows, normed], axis=0).astype(jnp.float32)
    conv_sum = jnp.zeros((tok_count, model_width), jnp.float32)
    for offset in range(kernel):
        conv_sum = conv_sum + conv_weight[offset] * padded[offset : offset + tok_count]
    conv_out = jax.nn.silu(conv_sum + conv_bias).astype(jnp.bfloat16)
    projected = jnp.dot(conv_out, proj_weight, preferred_element_type=jnp.float32)
    low_rank = projected[:, :low_width].astype(jnp.bfloat16)
    step_size = jax.nn.softplus(
        jnp.dot(low_rank, dt_weight, preferred_element_type=jnp.float32) + dt_bias
    )
    input_map = projected[:, low_width : low_width + states]
    output_map = projected[:, low_width + states :]
    decay_neg = -decay_rate
    conv_float = conv_out.astype(jnp.float32)
    lanes = 128
    rows = model_width // lanes
    chunks = 2
    count = rows // chunks
    drive = step_size * conv_float
    step3 = step_size.reshape(tok_count, rows, lanes)
    drive3 = drive.reshape(tok_count, rows, lanes)
    decay3 = decay_neg.reshape(states, rows, lanes)
    span3 = jnp.exp(decay_neg * jnp.sum(step_size, axis=0)[None, :]).reshape(states, rows, lanes)
    zero_state = jnp.zeros((states, count, lanes), jnp.float32)
    peers = lax.axis_size("seq")
    inflow = []
    for c in range(chunks):
        _, end_state = local_scan(
            zero_state, step3, drive3, input_map, output_map, decay3, False, c * count, count
        )
        summary = jnp.stack([span3[:, c * count : (c + 1) * count], end_state])
        inflow.append([from_behind(summary, "seq", k) for k in range(peers - 1, 0, -1)])
    pieces = []
    for c in range(chunks):
        incoming = jnp.zeros_like(zero_state)
        for piece in inflow[c]:
            incoming = piece[0] * incoming + piece[1]
        part, _ = local_scan(
            incoming, step3, drive3, input_map, output_map, decay3, True, c * count, count
        )
        pieces.append(part)
    scanned = jnp.concatenate(pieces, axis=1).reshape(tok_count, model_width)
    hidden_state = stream + (scanned + skip_gain * conv_float)
    ffn_in = rms_scale(hidden_state, ffn_gain).astype(jnp.bfloat16)
    owners = lax.axis_size("expert")
    experts = owners * w_gate.shape[0]
    capacity = 4 * tok_count // owners
    chosen = expert_ids[0].reshape(-1)
    onehot = (chosen[:, None] == jnp.arange(experts, dtype=jnp.int32)[None, :]).astype(jnp.int32)
    before = jnp.cumsum(onehot, axis=0) - onehot
    slot_pos = jnp.sum(before * onehot, axis=1)
    dest_row = chosen * capacity + slot_pos
    slot_ids = jnp.arange(experts * capacity, dtype=jnp.int32)
    pair_rows = dest_row.reshape(tok_count, 2)
    place_map = (
        (slot_ids[:, None] == pair_rows[None, :, 0]) | (slot_ids[:, None] == pair_rows[None, :, 1])
    ).astype(jnp.bfloat16)
    outgoing = jnp.dot(place_map, ffn_in, preferred_element_type=jnp.float32).astype(jnp.bfloat16)
    outgoing = outgoing.reshape(experts, capacity, model_width)
    received = lax.all_to_all(outgoing, "expert", split_axis=0, concat_axis=0, tiled=True)
    recv_shape = received.shape
    rows_in = received.reshape(-1, model_width)
    gate_part = jnp.dot(rows_in, w_gate[0], preferred_element_type=jnp.float32)
    up_part = jnp.dot(rows_in, w_up[0], preferred_element_type=jnp.float32)
    inner_act = (jax.nn.silu(gate_part) * up_part).astype(jnp.bfloat16)
    result = jnp.dot(inner_act, w_down[0], preferred_element_type=jnp.float32).astype(jnp.bfloat16)
    returned = lax.all_to_all(
        result.reshape(recv_shape), "expert", split_axis=0, concat_axis=0, tiled=True
    )
    flat_back = returned.reshape(experts * capacity, model_width)
    picks = [
        jnp.dot(
            (pair_rows[:, k][:, None] == slot_ids[None, :]).astype(jnp.bfloat16),
            flat_back,
            preferred_element_type=jnp.float32,
        )
        for k in range(2)
    ]
    route_scale = route_weights[0]
    routed = route_scale[:, 0:1] * picks[0] + route_scale[:, 1:2] * picks[1]
    block_out = (hidden_state + routed).astype(jnp.bfloat16)
    return block_out[None]


def solution(mesh):
    in_specs = (
        P("expert", "seq", None),
        P(),
        P(),
        P(),
        P(),
        P(),
        P(),
        P(),
        P(),
        P(),
        P("expert", "seq", None),
        P("expert", "seq", None),
        P("expert", None, None),
        P("expert", None, None),
        P("expert", None, None),
    )
    out_specs = P("expert", "seq", None)
    return jax.shard_map(
        per_device, mesh=mesh, in_specs=in_specs, out_specs=out_specs, check_vma=False
    )
```

```python
import functools

import jax
import jax.numpy as jnp
from jax import lax
from jax.sharding import PartitionSpec as P
from jax.experimental import pallas as pl
from jax.experimental.pallas import tpu as pltpu


MESH = pl.DeviceIdType.MESH


def exchange_kernel(peers, x_ref, o_ref, send_sems, recv_sems, local_sem):
    me = lax.axis_index("expert")
    row = lax.axis_index("seq")
    barrier = pltpu.get_barrier_semaphore()

    def signal(s, carry):
        peer = lax.rem(me + s, peers)
        pl.semaphore_signal(barrier, inc=1, device_id=(row, peer), device_id_type=MESH)
        return carry

    lax.fori_loop(1, peers, signal, 0)
    pl.semaphore_wait(barrier, peers - 1)
    local = pltpu.make_async_copy(x_ref.at[me], o_ref.at[me], local_sem)
    local.start()

    def send(s, carry):
        peer = lax.rem(me + s, peers)
        pltpu.make_async_remote_copy(
            src_ref=x_ref.at[peer],
            dst_ref=o_ref.at[me],
            send_sem=send_sems.at[peer],
            recv_sem=recv_sems.at[me],
            device_id=(row, peer),
            device_id_type=MESH,
        ).start()
        return carry

    lax.fori_loop(1, peers, send, 0)

    def finish(s, carry):
        peer = lax.rem(me + s, peers)
        pltpu.make_async_remote_copy(
            src_ref=x_ref.at[peer],
            dst_ref=o_ref.at[me],
            send_sem=send_sems.at[peer],
            recv_sem=recv_sems.at[me],
            device_id=(row, peer),
            device_id_type=MESH,
        ).wait_send()
        pltpu.make_async_remote_copy(
            src_ref=x_ref.at[me],
            dst_ref=o_ref.at[peer],
            send_sem=send_sems.at[me],
            recv_sem=recv_sems.at[peer],
            device_id=(row, peer),
            device_id_type=MESH,
        ).wait_recv()
        return carry

    lax.fori_loop(1, peers, finish, 0)
    local.wait()


def exchange(blocks, tag):
    peers = blocks.shape[0]
    return pl.pallas_call(
        functools.partial(exchange_kernel, peers),
        out_shape=jax.ShapeDtypeStruct(blocks.shape, blocks.dtype),
        in_specs=[pl.BlockSpec(memory_space=pl.ANY)],
        out_specs=pl.BlockSpec(memory_space=pl.ANY),
        scratch_shapes=[
            pltpu.SemaphoreType.DMA((peers,)),
            pltpu.SemaphoreType.DMA((peers,)),
            pltpu.SemaphoreType.DMA,
        ],
        compiler_params=pltpu.CompilerParams(collective_id=tag, has_side_effects=True),
    )(blocks)


def from_behind(array, axis, by):
    peers = lax.axis_size(axis)
    pairs = [(i, i + by) for i in range(peers) if 0 <= i + by < peers]
    return lax.ppermute(array, axis, pairs)


def prefix(array, axis, combine, identity):
    peers, place = (lax.axis_size(axis), lax.axis_index(axis))
    everything = jax.tree.map(lambda part: lax.all_gather(part, axis), array)
    start = jax.tree.map(
        lambda part, zero: jnp.broadcast_to(jnp.asarray(zero, part.dtype), part.shape),
        array,
        identity,
    )

    def turn(k, before):
        reached = k < place
        new = combine(before, jax.tree.map(lambda part: part[k], everything))
        return jax.tree.map(lambda a, b: jnp.where(reached, a, b), new, before)

    return lax.fori_loop(0, peers, turn, start)


def rms_scale(values, gain):
    return values * lax.rsqrt(jnp.mean(values * values, axis=-1, keepdims=True) + 1e-05) * gain


def scan_kernel(with_output):
    def body(in_ref, out_ref, step_ref, drive_ref, decay_ref, init_ref, *outs):
        states = decay_ref.shape[0]
        tok_count = step_ref.shape[0]
        decay_rows = [decay_ref[n] for n in range(states)]
        if with_output:
            y_ref, end_ref = outs
        else:
            (end_ref,) = outs

        def turn(t, carry):
            step_now = step_ref[t]
            drive_now = drive_ref[t]
            base = t * states
            total = None
            fresh = []
            for n in range(states):
                value = jnp.exp(step_now * decay_rows[n]) * carry[n] + drive_now * in_ref[base + n]
                fresh.append(value)
                if with_output:
                    part = out_ref[base + n] * value
                    total = part if total is None else total + part
            if with_output:
                y_ref[t] = total
            return tuple(fresh)

        start = tuple(init_ref[n] for n in range(states))
        final = lax.fori_loop(0, tok_count, turn, start, unroll=2)
        for n in range(states):
            end_ref[n] = final[n]

    return body


def local_scan(start_state, step3, drive3, input_map, output_map, decay3, with_output, first, count):
    tok_count, rows, lanes = step3.shape
    states = decay3.shape[0]
    blk = 8
    grid_len = count // blk
    lead = first // blk
    smem = pl.BlockSpec(memory_space=pltpu.SMEM)
    seq_spec = pl.BlockSpec((tok_count, blk, lanes), lambda j: (0, j + lead, 0))
    st_spec = pl.BlockSpec((states, blk, lanes), lambda j: (0, j + lead, 0))
    own_seq = pl.BlockSpec((tok_count, blk, lanes), lambda j: (0, j, 0))
    own_st = pl.BlockSpec((states, blk, lanes), lambda j: (0, j, 0))
    out_shape = [jax.ShapeDtypeStruct((states, count, lanes), jnp.float32)]
    out_specs = [own_st]
    if with_output:
        out_shape.insert(0, jax.ShapeDtypeStruct((tok_count, count, lanes), jnp.float32))
        out_specs.insert(0, own_seq)
    results = pl.pallas_call(
        scan_kernel(with_output),
        grid=(grid_len,),
        in_specs=[smem, smem, seq_spec, seq_spec, st_spec, own_st],
        out_specs=out_specs,
        out_shape=out_shape,
    )(input_map.reshape(-1), output_map.reshape(-1), step3, drive3, decay3, start_state)
    if with_output:
        return (results[0], results[-1])
    return (None, results[-1])


def per_device(
    tokens,
    norm_gain,
    conv_weight,
    conv_bias,
    proj_weight,
    dt_weight,
    dt_bias,
    decay_rate,
    skip_gain,
    ffn_gain,
    expert_ids,
    route_weights,
    w_gate,
    w_up,
    w_down,
):
    stream = tokens[0].astype(jnp.float32)
    tok_count = stream.shape[0]
    model_width = stream.shape[1]
    kernel = conv_weight.shape[0]
    low_width = dt_weight.shape[0]
    states = decay_rate.shape[0]
    normed = rms_scale(stream, norm_gain).astype(jnp.bfloat16)
    prior_rows = from_behind(normed[tok_count - (kernel - 1) :], "seq", 1)
    padded = jnp.concatenate([prior_rows, normed], axis=0).astype(jnp.float32)
    conv_sum = jnp.zeros((tok_count, model_width), jnp.float32)
    for offset in range(kernel):
        conv_sum = conv_sum + conv_weight[offset] * padded[offset : offset + tok_count]
    conv_out = jax.nn.silu(conv_sum + conv_bias).astype(jnp.bfloat16)
    projected = jnp.dot(conv_out, proj_weight, preferred_element_type=jnp.float32)
    low_rank = projected[:, :low_width].astype(jnp.bfloat16)
    step_size = jax.nn.softplus(
        jnp.dot(low_rank, dt_weight, preferred_element_type=jnp.float32) + dt_bias
    )
    input_map = projected[:, low_width : low_width + states]
    output_map = projected[:, low_width + states :]
    decay_neg = -decay_rate
    conv_float = conv_out.astype(jnp.float32)
    lanes = 128
    rows = model_width // lanes
    chunks = 2
    count = rows // chunks
    drive = step_size * conv_float
    step3 = step_size.reshape(tok_count, rows, lanes)
    drive3 = drive.reshape(tok_count, rows, lanes)
    decay3 = decay_neg.reshape(states, rows, lanes)
    span3 = jnp.exp(decay_neg * jnp.sum(step_size, axis=0)[None, :]).reshape(states, rows, lanes)
    zero_state = jnp.zeros((states, count, lanes), jnp.float32)
    peers = lax.axis_size("seq")
    inflow = []
    for c in range(chunks):
        _, end_state = local_scan(
            zero_state, step3, drive3, input_map, output_map, decay3, False, c * count, count
        )
        summary = jnp.stack([span3[:, c * count : (c + 1) * count], end_state])
        inflow.append([from_behind(summary, "seq", k) for k in range(peers - 1, 0, -1)])
    pieces = []
    for c in range(chunks):
        incoming = jnp.zeros_like(zero_state)
        for piece in inflow[c]:
            incoming = piece[0] * incoming + piece[1]
        part, _ = local_scan(
            incoming, step3, drive3, input_map, output_map, decay3, True, c * count, count
        )
        pieces.append(part)
    scanned = jnp.concatenate(pieces, axis=1).reshape(tok_count, model_width)
    hidden_state = stream + (scanned + skip_gain * conv_float)
    ffn_in = rms_scale(hidden_state, ffn_gain).astype(jnp.bfloat16)
    owners = lax.axis_size("expert")
    experts = owners * w_gate.shape[0]
    capacity = 4 * tok_count // owners
    chosen = expert_ids[0].reshape(-1)
    onehot = (chosen[:, None] == jnp.arange(experts, dtype=jnp.int32)[None, :]).astype(jnp.int32)
    before = jnp.cumsum(onehot, axis=0) - onehot
    slot_pos = jnp.sum(before * onehot, axis=1)
    dest_row = chosen * capacity + slot_pos
    slot_ids = jnp.arange(experts * capacity, dtype=jnp.int32)
    pair_rows = dest_row.reshape(tok_count, 2)
    place_map = (
        (slot_ids[:, None] == pair_rows[None, :, 0]) | (slot_ids[:, None] == pair_rows[None, :, 1])
    ).astype(jnp.bfloat16)
    outgoing = jnp.dot(place_map, ffn_in, preferred_element_type=jnp.float32).astype(jnp.bfloat16)
    outgoing = outgoing.reshape(experts, capacity, model_width)
    received = exchange(outgoing, 0)
    recv_shape = received.shape
    rows_in = received.reshape(-1, model_width)
    gate_part = jnp.dot(rows_in, w_gate[0], preferred_element_type=jnp.float32)
    up_part = jnp.dot(rows_in, w_up[0], preferred_element_type=jnp.float32)
    inner_act = (jax.nn.silu(gate_part) * up_part).astype(jnp.bfloat16)
    result = jnp.dot(inner_act, w_down[0], preferred_element_type=jnp.float32).astype(jnp.bfloat16)
    returned = exchange(result.reshape(recv_shape), 1)
    flat_back = returned.reshape(experts * capacity, model_width)
    picks = [
        jnp.dot(
            (pair_rows[:, k][:, None] == slot_ids[None, :]).astype(jnp.bfloat16),
            flat_back,
            preferred_element_type=jnp.float32,
        )
        for k in range(2)
    ]
    route_scale = route_weights[0]
    routed = route_scale[:, 0:1] * picks[0] + route_scale[:, 1:2] * picks[1]
    block_out = (hidden_state + routed).astype(jnp.bfloat16)
    return block_out[None]


def solution(mesh):
    in_specs = (
        P("expert", "seq", None),
        P(),
        P(),
        P(),
        P(),
        P(),
        P(),
        P(),
        P(),
        P(),
        P("expert", "seq", None),
        P("expert", "seq", None),
        P("expert", None, None),
        P("expert", None, None),
        P("expert", None, None),
    )
    out_specs = P("expert", "seq", None)
    return jax.shard_map(
        per_device, mesh=mesh, in_specs=in_specs, out_specs=out_specs, check_vma=False
    )
```

```python
import jax
import jax.numpy as jnp
from jax import lax
from jax.sharding import PartitionSpec as P
from jax.experimental import pallas as pl
from jax.experimental.pallas import tpu as pltpu


def from_behind(array, axis, by):
    peers = lax.axis_size(axis)
    pairs = [(i, i + by) for i in range(peers) if 0 <= i + by < peers]
    return lax.ppermute(array, axis, pairs)


def prefix(array, axis, combine, identity):
    peers, place = (lax.axis_size(axis), lax.axis_index(axis))
    everything = jax.tree.map(lambda part: lax.all_gather(part, axis), array)
    start = jax.tree.map(
        lambda part, zero: jnp.broadcast_to(jnp.asarray(zero, part.dtype), part.shape),
        array,
        identity,
    )

    def turn(k, before):
        reached = k < place
        new = combine(before, jax.tree.map(lambda part: part[k], everything))
        return jax.tree.map(lambda a, b: jnp.where(reached, a, b), new, before)

    return lax.fori_loop(0, peers, turn, start)


def rms_scale(values, gain):
    return values * lax.rsqrt(jnp.mean(values * values, axis=-1, keepdims=True) + 1e-05) * gain


def scan_kernel(with_output):
    def body(in_ref, out_ref, step_ref, drive_ref, decay_ref, init_ref, *outs):
        states = decay_ref.shape[0]
        tok_count = step_ref.shape[0]
        decay_rows = [decay_ref[n] for n in range(states)]
        if with_output:
            y_ref, end_ref = outs
        else:
            (end_ref,) = outs

        def turn(t, carry):
            step_now = step_ref[t]
            drive_now = drive_ref[t]
            base = t * states
            total = None
            fresh = []
            for n in range(states):
                value = jnp.exp(step_now * decay_rows[n]) * carry[n] + drive_now * in_ref[base + n]
                fresh.append(value)
                if with_output:
                    part = out_ref[base + n] * value
                    total = part if total is None else total + part
            if with_output:
                y_ref[t] = total
            return tuple(fresh)

        start = tuple(init_ref[n] for n in range(states))
        final = lax.fori_loop(0, tok_count, turn, start, unroll=2)
        for n in range(states):
            end_ref[n] = final[n]

    return body


def local_scan(start_state, step3, drive3, input_map, output_map, decay3, with_output, first, count):
    tok_count, rows, lanes = step3.shape
    states = decay3.shape[0]
    blk = 8
    grid_len = count // blk
    lead = first // blk
    smem = pl.BlockSpec(memory_space=pltpu.SMEM)
    seq_spec = pl.BlockSpec((tok_count, blk, lanes), lambda j: (0, j + lead, 0))
    st_spec = pl.BlockSpec((states, blk, lanes), lambda j: (0, j + lead, 0))
    own_seq = pl.BlockSpec((tok_count, blk, lanes), lambda j: (0, j, 0))
    own_st = pl.BlockSpec((states, blk, lanes), lambda j: (0, j, 0))
    out_shape = [jax.ShapeDtypeStruct((states, count, lanes), jnp.float32)]
    out_specs = [own_st]
    if with_output:
        out_shape.insert(0, jax.ShapeDtypeStruct((tok_count, count, lanes), jnp.float32))
        out_specs.insert(0, own_seq)
    results = pl.pallas_call(
        scan_kernel(with_output),
        grid=(grid_len,),
        in_specs=[smem, smem, seq_spec, seq_spec, st_spec, own_st],
        out_specs=out_specs,
        out_shape=out_shape,
    )(input_map.reshape(-1), output_map.reshape(-1), step3, drive3, decay3, start_state)
    if with_output:
        return (results[0], results[-1])
    return (None, results[-1])


def per_device(
    tokens,
    norm_gain,
    conv_weight,
    conv_bias,
    proj_weight,
    dt_weight,
    dt_bias,
    decay_rate,
    skip_gain,
    ffn_gain,
    expert_ids,
    route_weights,
    w_gate,
    w_up,
    w_down,
):
    stream = tokens[0].astype(jnp.float32)
    tok_count = stream.shape[0]
    model_width = stream.shape[1]
    kernel = conv_weight.shape[0]
    low_width = dt_weight.shape[0]
    states = decay_rate.shape[0]
    normed = rms_scale(stream, norm_gain).astype(jnp.bfloat16)
    prior_rows = from_behind(normed[tok_count - (kernel - 1) :], "seq", 1)
    padded = jnp.concatenate([prior_rows, normed], axis=0).astype(jnp.float32)
    conv_sum = jnp.zeros((tok_count, model_width), jnp.float32)
    for offset in range(kernel):
        conv_sum = conv_sum + conv_weight[offset] * padded[offset : offset + tok_count]
    conv_out = jax.nn.silu(conv_sum + conv_bias).astype(jnp.bfloat16)
    projected = jnp.dot(conv_out, proj_weight, preferred_element_type=jnp.float32)
    low_rank = projected[:, :low_width].astype(jnp.bfloat16)
    step_size = jax.nn.softplus(
        jnp.dot(low_rank, dt_weight, preferred_element_type=jnp.float32) + dt_bias
    )
    input_map = projected[:, low_width : low_width + states]
    output_map = projected[:, low_width + states :]
    decay_neg = -decay_rate
    conv_float = conv_out.astype(jnp.float32)
    lanes = 128
    rows = model_width // lanes
    chunks = 2
    count = rows // chunks
    drive = step_size * conv_float
    step3 = step_size.reshape(tok_count, rows, lanes)
    drive3 = drive.reshape(tok_count, rows, lanes)
    decay3 = decay_neg.reshape(states, rows, lanes)
    span3 = jnp.exp(decay_neg * jnp.sum(step_size, axis=0)[None, :]).reshape(states, rows, lanes)
    zero_state = jnp.zeros((states, count, lanes), jnp.float32)
    peers = lax.axis_size("seq")
    inflow = []
    for c in range(chunks):
        _, end_state = local_scan(
            zero_state, step3, drive3, input_map, output_map, decay3, False, c * count, count
        )
        summary = jnp.stack([span3[:, c * count : (c + 1) * count], end_state])
        inflow.append([from_behind(summary, "seq", k) for k in range(peers - 1, 0, -1)])
    pieces = []
    for c in range(chunks):
        incoming = jnp.zeros_like(zero_state)
        for piece in inflow[c]:
            incoming = piece[0] * incoming + piece[1]
        part, _ = local_scan(
            incoming, step3, drive3, input_map, output_map, decay3, True, c * count, count
        )
        pieces.append(part)
    scanned = jnp.concatenate(pieces, axis=1).reshape(tok_count, model_width)
    hidden_state = stream + (scanned + skip_gain * conv_float)
    ffn_in = rms_scale(hidden_state, ffn_gain).astype(jnp.bfloat16)
    owners = lax.axis_size("expert")
    experts = owners * w_gate.shape[0]
    capacity = 4 * tok_count // owners
    chosen = expert_ids[0].reshape(-1)
    onehot = (chosen[:, None] == jnp.arange(experts, dtype=jnp.int32)[None, :]).astype(jnp.int32)
    before = jnp.cumsum(onehot, axis=0) - onehot
    slot_pos = jnp.sum(before * onehot, axis=1)
    dest_row = chosen * capacity + slot_pos
    slot_ids = jnp.arange(experts * capacity, dtype=jnp.int32)
    pair_rows = dest_row.reshape(tok_count, 2)
    place_map = (
        (slot_ids[:, None] == pair_rows[None, :, 0]) | (slot_ids[:, None] == pair_rows[None, :, 1])
    ).astype(jnp.bfloat16)
    halves = 2
    part_cap = capacity // halves
    place_parts = place_map.reshape(experts, halves, part_cap, tok_count)
    pick_maps = [
        (pair_rows[:, k][:, None] == slot_ids[None, :])
        .astype(jnp.bfloat16)
        .reshape(tok_count, experts, halves, part_cap)
        for k in range(2)
    ]
    picks = [None, None]
    for h in range(halves):
        place_h = place_parts[:, h].reshape(experts * part_cap, tok_count)
        outgoing = jnp.dot(place_h, ffn_in, preferred_element_type=jnp.float32).astype(jnp.bfloat16)
        outgoing = outgoing.reshape(experts, part_cap, model_width)
        received = lax.all_to_all(outgoing, "expert", split_axis=0, concat_axis=0, tiled=True)
        rows_in = received.reshape(-1, model_width)
        gate_part = jnp.dot(rows_in, w_gate[0], preferred_element_type=jnp.float32)
        up_part = jnp.dot(rows_in, w_up[0], preferred_element_type=jnp.float32)
        inner_act = (jax.nn.silu(gate_part) * up_part).astype(jnp.bfloat16)
        result = jnp.dot(inner_act, w_down[0], preferred_element_type=jnp.float32).astype(
            jnp.bfloat16
        )
        returned = lax.all_to_all(
            result.reshape(experts, part_cap, model_width),
            "expert",
            split_axis=0,
            concat_axis=0,
            tiled=True,
        )
        flat_back = returned.reshape(experts * part_cap, model_width)
        for k in range(2):
            got = jnp.dot(
                pick_maps[k][:, :, h].reshape(tok_count, experts * part_cap),
                flat_back,
                preferred_element_type=jnp.float32,
            )
            picks[k] = got if picks[k] is None else picks[k] + got
    route_scale = route_weights[0]
    routed = route_scale[:, 0:1] * picks[0] + route_scale[:, 1:2] * picks[1]
    block_out = (hidden_state + routed).astype(jnp.bfloat16)
    return block_out[None]


def solution(mesh):
    in_specs = (
        P("expert", "seq", None),
        P(),
        P(),
        P(),
        P(),
        P(),
        P(),
        P(),
        P(),
        P(),
        P("expert", "seq", None),
        P("expert", "seq", None),
        P("expert", None, None),
        P("expert", None, None),
        P("expert", None, None),
    )
    out_specs = P("expert", "seq", None)
    return jax.shard_map(
        per_device, mesh=mesh, in_specs=in_specs, out_specs=out_specs, check_vma=False
    )
```

```python
import jax
import jax.numpy as jnp
from jax import lax
from jax.sharding import PartitionSpec as P
from jax.experimental import pallas as pl
from jax.experimental.pallas import tpu as pltpu


def from_behind(array, axis, by):
    peers = lax.axis_size(axis)
    pairs = [(i, i + by) for i in range(peers) if 0 <= i + by < peers]
    return lax.ppermute(array, axis, pairs)


def prefix(array, axis, combine, identity):
    peers, place = (lax.axis_size(axis), lax.axis_index(axis))
    everything = jax.tree.map(lambda part: lax.all_gather(part, axis), array)
    start = jax.tree.map(
        lambda part, zero: jnp.broadcast_to(jnp.asarray(zero, part.dtype), part.shape),
        array,
        identity,
    )

    def turn(k, before):
        reached = k < place
        new = combine(before, jax.tree.map(lambda part: part[k], everything))
        return jax.tree.map(lambda a, b: jnp.where(reached, a, b), new, before)

    return lax.fori_loop(0, peers, turn, start)


def rms_scale(values, gain):
    return values * lax.rsqrt(jnp.mean(values * values, axis=-1, keepdims=True) + 1e-05) * gain


def scan_kernel(with_output):
    def body(in_ref, out_ref, step_ref, drive_ref, decay_ref, init_ref, *outs):
        states = decay_ref.shape[0]
        tok_count = step_ref.shape[0]
        decay_rows = [decay_ref[n] for n in range(states)]
        if with_output:
            y_ref, end_ref = outs
        else:
            (end_ref,) = outs

        def turn(t, carry):
            step_now = step_ref[t]
            drive_now = drive_ref[t]
            base = t * states
            total = None
            fresh = []
            for n in range(states):
                value = jnp.exp(step_now * decay_rows[n]) * carry[n] + drive_now * in_ref[base + n]
                fresh.append(value)
                if with_output:
                    part = out_ref[base + n] * value
                    total = part if total is None else total + part
            if with_output:
                y_ref[t] = total
            return tuple(fresh)

        start = tuple(init_ref[n] for n in range(states))
        final = lax.fori_loop(0, tok_count, turn, start, unroll=8)
        for n in range(states):
            end_ref[n] = final[n]

    return body


def local_scan(start_state, step3, drive3, input_map, output_map, decay3, with_output, first, count):
    tok_count, rows, lanes = step3.shape
    states = decay3.shape[0]
    blk = 8
    grid_len = count // blk
    lead = first // blk
    smem = pl.BlockSpec(memory_space=pltpu.SMEM)
    seq_spec = pl.BlockSpec((tok_count, blk, lanes), lambda j: (0, j + lead, 0))
    st_spec = pl.BlockSpec((states, blk, lanes), lambda j: (0, j + lead, 0))
    own_seq = pl.BlockSpec((tok_count, blk, lanes), lambda j: (0, j, 0))
    own_st = pl.BlockSpec((states, blk, lanes), lambda j: (0, j, 0))
    out_shape = [jax.ShapeDtypeStruct((states, count, lanes), jnp.float32)]
    out_specs = [own_st]
    if with_output:
        out_shape.insert(0, jax.ShapeDtypeStruct((tok_count, count, lanes), jnp.float32))
        out_specs.insert(0, own_seq)
    results = pl.pallas_call(
        scan_kernel(with_output),
        grid=(grid_len,),
        in_specs=[smem, smem, seq_spec, seq_spec, st_spec, own_st],
        out_specs=out_specs,
        out_shape=out_shape,
    )(input_map.reshape(-1), output_map.reshape(-1), step3, drive3, decay3, start_state)
    if with_output:
        return (results[0], results[-1])
    return (None, results[-1])


def per_device(
    tokens,
    norm_gain,
    conv_weight,
    conv_bias,
    proj_weight,
    dt_weight,
    dt_bias,
    decay_rate,
    skip_gain,
    ffn_gain,
    expert_ids,
    route_weights,
    w_gate,
    w_up,
    w_down,
):
    stream = tokens[0].astype(jnp.float32)
    tok_count = stream.shape[0]
    model_width = stream.shape[1]
    kernel = conv_weight.shape[0]
    low_width = dt_weight.shape[0]
    states = decay_rate.shape[0]
    normed = rms_scale(stream, norm_gain).astype(jnp.bfloat16)
    prior_rows = from_behind(normed[tok_count - (kernel - 1) :], "seq", 1)
    padded = jnp.concatenate([prior_rows, normed], axis=0).astype(jnp.float32)
    conv_sum = jnp.zeros((tok_count, model_width), jnp.float32)
    for offset in range(kernel):
        conv_sum = conv_sum + conv_weight[offset] * padded[offset : offset + tok_count]
    conv_out = jax.nn.silu(conv_sum + conv_bias).astype(jnp.bfloat16)
    projected = jnp.dot(conv_out, proj_weight, preferred_element_type=jnp.float32)
    low_rank = projected[:, :low_width].astype(jnp.bfloat16)
    step_size = jax.nn.softplus(
        jnp.dot(low_rank, dt_weight, preferred_element_type=jnp.float32) + dt_bias
    )
    input_map = projected[:, low_width : low_width + states]
    output_map = projected[:, low_width + states :]
    decay_neg = -decay_rate
    conv_float = conv_out.astype(jnp.float32)
    lanes = 128
    rows = model_width // lanes
    chunks = 2
    count = rows // chunks
    drive = step_size * conv_float
    step3 = step_size.reshape(tok_count, rows, lanes)
    drive3 = drive.reshape(tok_count, rows, lanes)
    decay3 = decay_neg.reshape(states, rows, lanes)
    span3 = jnp.exp(decay_neg * jnp.sum(step_size, axis=0)[None, :]).reshape(states, rows, lanes)
    zero_state = jnp.zeros((states, count, lanes), jnp.float32)
    peers = lax.axis_size("seq")
    inflow = []
    for c in range(chunks):
        _, end_state = local_scan(
            zero_state, step3, drive3, input_map, output_map, decay3, False, c * count, count
        )
        summary = jnp.stack([span3[:, c * count : (c + 1) * count], end_state])
        inflow.append([from_behind(summary, "seq", k) for k in range(peers - 1, 0, -1)])
    pieces = []
    for c in range(chunks):
        incoming = jnp.zeros_like(zero_state)
        for piece in inflow[c]:
            incoming = piece[0] * incoming + piece[1]
        part, _ = local_scan(
            incoming, step3, drive3, input_map, output_map, decay3, True, c * count, count
        )
        pieces.append(part)
    scanned = jnp.concatenate(pieces, axis=1).reshape(tok_count, model_width)
    hidden_state = stream + (scanned + skip_gain * conv_float)
    ffn_in = rms_scale(hidden_state, ffn_gain).astype(jnp.bfloat16)
    owners = lax.axis_size("expert")
    experts = owners * w_gate.shape[0]
    capacity = 4 * tok_count // owners
    chosen = expert_ids[0].reshape(-1)
    onehot = (chosen[:, None] == jnp.arange(experts, dtype=jnp.int32)[None, :]).astype(jnp.int32)
    before = jnp.cumsum(onehot, axis=0) - onehot
    slot_pos = jnp.sum(before * onehot, axis=1)
    dest_row = chosen * capacity + slot_pos
    slot_ids = jnp.arange(experts * capacity, dtype=jnp.int32)
    pair_rows = dest_row.reshape(tok_count, 2)
    place_map = (
        (slot_ids[:, None] == pair_rows[None, :, 0]) | (slot_ids[:, None] == pair_rows[None, :, 1])
    ).astype(jnp.bfloat16)
    outgoing = jnp.dot(place_map, ffn_in, preferred_element_type=jnp.float32).astype(jnp.bfloat16)
    outgoing = outgoing.reshape(experts, capacity, model_width)
    received = lax.all_to_all(outgoing, "expert", split_axis=0, concat_axis=0, tiled=True)
    recv_shape = received.shape
    rows_in = received.reshape(-1, model_width)
    gate_part = jnp.dot(rows_in, w_gate[0], preferred_element_type=jnp.float32)
    up_part = jnp.dot(rows_in, w_up[0], preferred_element_type=jnp.float32)
    inner_act = (jax.nn.silu(gate_part) * up_part).astype(jnp.bfloat16)
    result = jnp.dot(inner_act, w_down[0], preferred_element_type=jnp.float32).astype(jnp.bfloat16)
    returned = lax.all_to_all(
        result.reshape(recv_shape), "expert", split_axis=0, concat_axis=0, tiled=True
    )
    flat_back = returned.reshape(experts * capacity, model_width)
    picks = [
        jnp.dot(
            (pair_rows[:, k][:, None] == slot_ids[None, :]).astype(jnp.bfloat16),
            flat_back,
            preferred_element_type=jnp.float32,
        )
        for k in range(2)
    ]
    route_scale = route_weights[0]
    routed = route_scale[:, 0:1] * picks[0] + route_scale[:, 1:2] * picks[1]
    block_out = (hidden_state + routed).astype(jnp.bfloat16)
    return block_out[None]


def solution(mesh):
    in_specs = (
        P("expert", "seq", None),
        P(),
        P(),
        P(),
        P(),
        P(),
        P(),
        P(),
        P(),
        P(),
        P("expert", "seq", None),
        P("expert", "seq", None),
        P("expert", None, None),
        P("expert", None, None),
        P("expert", None, None),
    )
    out_specs = P("expert", "seq", None)
    return jax.shard_map(
        per_device, mesh=mesh, in_specs=in_specs, out_specs=out_specs, check_vma=False
    )
```

```python
import jax
import jax.numpy as jnp
from jax import lax
from jax.sharding import PartitionSpec as P
from jax.experimental import pallas as pl
from jax.experimental.pallas import tpu as pltpu


def from_behind(array, axis, by):
    peers = lax.axis_size(axis)
    pairs = [(i, i + by) for i in range(peers) if 0 <= i + by < peers]
    return lax.ppermute(array, axis, pairs)


def prefix(array, axis, combine, identity):
    peers, place = (lax.axis_size(axis), lax.axis_index(axis))
    everything = jax.tree.map(lambda part: lax.all_gather(part, axis), array)
    start = jax.tree.map(
        lambda part, zero: jnp.broadcast_to(jnp.asarray(zero, part.dtype), part.shape),
        array,
        identity,
    )

    def turn(k, before):
        reached = k < place
        new = combine(before, jax.tree.map(lambda part: part[k], everything))
        return jax.tree.map(lambda a, b: jnp.where(reached, a, b), new, before)

    return lax.fori_loop(0, peers, turn, start)


def rms_scale(values, gain):
    return values * lax.rsqrt(jnp.mean(values * values, axis=-1, keepdims=True) + 1e-05) * gain


def scan_kernel(with_output):
    def body(in_ref, out_ref, step_ref, drive_ref, decay_ref, init_ref, *outs):
        states = decay_ref.shape[0]
        tok_count = step_ref.shape[0]
        decay_rows = [decay_ref[n] for n in range(states)]
        if with_output:
            y_ref, end_ref = outs
        else:
            (end_ref,) = outs

        def turn(t, carry):
            step_now = step_ref[t]
            drive_now = drive_ref[t]
            base = t * states
            total = None
            fresh = []
            for n in range(states):
                value = jnp.exp(step_now * decay_rows[n]) * carry[n] + drive_now * in_ref[base + n]
                fresh.append(value)
                if with_output:
                    part = out_ref[base + n] * value
                    total = part if total is None else total + part
            if with_output:
                y_ref[t] = total
            return tuple(fresh)

        start = tuple(init_ref[n] for n in range(states))
        final = lax.fori_loop(0, tok_count, turn, start, unroll=8)
        for n in range(states):
            end_ref[n] = final[n]

    return body


def local_scan(start_state, step3, drive3, input_map, output_map, decay3, with_output, first, count):
    tok_count, rows, lanes = step3.shape
    states = decay3.shape[0]
    blk = 8
    grid_len = count // blk
    lead = first // blk
    smem = pl.BlockSpec(memory_space=pltpu.SMEM)
    seq_spec = pl.BlockSpec((tok_count, blk, lanes), lambda j: (0, j + lead, 0))
    st_spec = pl.BlockSpec((states, blk, lanes), lambda j: (0, j + lead, 0))
    own_seq = pl.BlockSpec((tok_count, blk, lanes), lambda j: (0, j, 0))
    own_st = pl.BlockSpec((states, blk, lanes), lambda j: (0, j, 0))
    out_shape = [jax.ShapeDtypeStruct((states, count, lanes), jnp.float32)]
    out_specs = [own_st]
    if with_output:
        out_shape.insert(0, jax.ShapeDtypeStruct((tok_count, count, lanes), jnp.float32))
        out_specs.insert(0, own_seq)
    results = pl.pallas_call(
        scan_kernel(with_output),
        grid=(grid_len,),
        in_specs=[smem, smem, seq_spec, seq_spec, st_spec, own_st],
        out_specs=out_specs,
        out_shape=out_shape,
    )(input_map.reshape(-1), output_map.reshape(-1), step3, drive3, decay3, start_state)
    if with_output:
        return (results[0], results[-1])
    return (None, results[-1])


def per_device(
    tokens,
    norm_gain,
    conv_weight,
    conv_bias,
    proj_weight,
    dt_weight,
    dt_bias,
    decay_rate,
    skip_gain,
    ffn_gain,
    expert_ids,
    route_weights,
    w_gate,
    w_up,
    w_down,
):
    stream = tokens[0].astype(jnp.float32)
    tok_count = stream.shape[0]
    model_width = stream.shape[1]
    kernel = conv_weight.shape[0]
    low_width = dt_weight.shape[0]
    states = decay_rate.shape[0]
    normed = rms_scale(stream, norm_gain).astype(jnp.bfloat16)
    prior_rows = from_behind(normed[tok_count - (kernel - 1) :], "seq", 1)
    padded = jnp.concatenate([prior_rows, normed], axis=0).astype(jnp.float32)
    conv_sum = jnp.zeros((tok_count, model_width), jnp.float32)
    for offset in range(kernel):
        conv_sum = conv_sum + conv_weight[offset] * padded[offset : offset + tok_count]
    conv_out = jax.nn.silu(conv_sum + conv_bias).astype(jnp.bfloat16)
    projected = jnp.dot(conv_out, proj_weight, preferred_element_type=jnp.float32)
    low_rank = projected[:, :low_width].astype(jnp.bfloat16)
    step_size = jax.nn.softplus(
        jnp.dot(low_rank, dt_weight, preferred_element_type=jnp.float32) + dt_bias
    )
    input_map = projected[:, low_width : low_width + states]
    output_map = projected[:, low_width + states :]
    decay_neg = -decay_rate
    conv_float = conv_out.astype(jnp.float32)
    lanes = 128
    rows = model_width // lanes
    chunks = 2
    count = rows // chunks
    drive = step_size * conv_float
    step3 = step_size.reshape(tok_count, rows, lanes)
    drive3 = drive.reshape(tok_count, rows, lanes)
    decay3 = decay_neg.reshape(states, rows, lanes)
    span3 = jnp.exp(decay_neg * jnp.sum(step_size, axis=0)[None, :]).reshape(states, rows, lanes)
    zero_state = jnp.zeros((states, count, lanes), jnp.float32)
    peers = lax.axis_size("seq")
    inflow = []
    for c in range(chunks):
        _, end_state = local_scan(
            zero_state, step3, drive3, input_map, output_map, decay3, False, c * count, count
        )
        summary = jnp.stack([span3[:, c * count : (c + 1) * count], end_state])
        inflow.append([from_behind(summary, "seq", k) for k in range(peers - 1, 0, -1)])
    pieces = []
    for c in range(chunks):
        incoming = jnp.zeros_like(zero_state)
        for piece in inflow[c]:
            incoming = piece[0] * incoming + piece[1]
        part, _ = local_scan(
            incoming, step3, drive3, input_map, output_map, decay3, True, c * count, count
        )
        pieces.append(part)
    scanned = jnp.concatenate(pieces, axis=1).reshape(tok_count, model_width)
    hidden_state = stream + (scanned + skip_gain * conv_float)
    ffn_in = rms_scale(hidden_state, ffn_gain).astype(jnp.bfloat16)
    owners = lax.axis_size("expert")
    experts = owners * w_gate.shape[0]
    capacity = 4 * tok_count // owners
    chosen = expert_ids[0].reshape(-1)
    onehot = (chosen[:, None] == jnp.arange(experts, dtype=jnp.int32)[None, :]).astype(jnp.int32)
    before = jnp.cumsum(onehot, axis=0) - onehot
    slot_pos = jnp.sum(before * onehot, axis=1)
    dest_row = chosen * capacity + slot_pos
    slot_ids = jnp.arange(experts * capacity, dtype=jnp.int32)
    pair_rows = dest_row.reshape(tok_count, 2)
    place_map = (
        (slot_ids[:, None] == pair_rows[None, :, 0]) | (slot_ids[:, None] == pair_rows[None, :, 1])
    ).astype(jnp.bfloat16)
    outgoing = jnp.dot(place_map, ffn_in, preferred_element_type=jnp.float32).astype(jnp.bfloat16)
    outgoing = outgoing.reshape(experts, capacity, model_width)
    received = lax.all_to_all(outgoing, "expert", split_axis=0, concat_axis=0, tiled=True)
    recv_shape = received.shape
    rows_in = received.reshape(-1, model_width)
    gate_part = jnp.dot(rows_in, w_gate[0], preferred_element_type=jnp.float32)
    up_part = jnp.dot(rows_in, w_up[0], preferred_element_type=jnp.float32)
    inner_act = (jax.nn.silu(gate_part) * up_part).astype(jnp.bfloat16)
    result = jnp.dot(inner_act, w_down[0], preferred_element_type=jnp.float32).astype(jnp.bfloat16)
    returned = lax.all_to_all(
        result.reshape(recv_shape), "expert", split_axis=0, concat_axis=0, tiled=True
    )
    flat_back = returned.reshape(experts * capacity, model_width)
    picks = [
        jnp.dot(
            (pair_rows[:, k][:, None] == slot_ids[None, :]).astype(jnp.bfloat16),
            flat_back,
            preferred_element_type=jnp.bfloat16,
        ).astype(jnp.float32)
        for k in range(2)
    ]
    route_scale = route_weights[0]
    routed = route_scale[:, 0:1] * picks[0] + route_scale[:, 1:2] * picks[1]
    block_out = (hidden_state + routed).astype(jnp.bfloat16)
    return block_out[None]


def solution(mesh):
    in_specs = (
        P("expert", "seq", None),
        P(),
        P(),
        P(),
        P(),
        P(),
        P(),
        P(),
        P(),
        P(),
        P("expert", "seq", None),
        P("expert", "seq", None),
        P("expert", None, None),
        P("expert", None, None),
        P("expert", None, None),
    )
    out_specs = P("expert", "seq", None)
    return jax.shard_map(
        per_device, mesh=mesh, in_specs=in_specs, out_specs=out_specs, check_vma=False
    )
```

```python
import math

import jax
import jax.numpy as jnp
from jax import lax
from jax.sharding import PartitionSpec as P
from jax.experimental import pallas as pl
from jax.experimental.pallas import tpu as pltpu


def from_behind(array, axis, by):
    peers = lax.axis_size(axis)
    pairs = [(i, i + by) for i in range(peers) if 0 <= i + by < peers]
    return lax.ppermute(array, axis, pairs)


def prefix(array, axis, combine, identity):
    peers, place = (lax.axis_size(axis), lax.axis_index(axis))
    everything = jax.tree.map(lambda part: lax.all_gather(part, axis), array)
    start = jax.tree.map(
        lambda part, zero: jnp.broadcast_to(jnp.asarray(zero, part.dtype), part.shape),
        array,
        identity,
    )

    def turn(k, before):
        reached = k < place
        new = combine(before, jax.tree.map(lambda part: part[k], everything))
        return jax.tree.map(lambda a, b: jnp.where(reached, a, b), new, before)

    return lax.fori_loop(0, peers, turn, start)


def rms_scale(values, gain):
    return values * lax.rsqrt(jnp.mean(values * values, axis=-1, keepdims=True) + 1e-05) * gain


def scan_kernel(with_output):
    def body(in_ref, out_ref, step_ref, drive_ref, decay_ref, init_ref, *outs):
        states = decay_ref.shape[0]
        tok_count = step_ref.shape[0]
        decay_rows = [decay_ref[n] for n in range(states)]
        if with_output:
            y_ref, end_ref = outs
        else:
            (end_ref,) = outs

        def turn(t, carry):
            step_now = step_ref[t]
            drive_now = drive_ref[t]
            base = t * states
            total = None
            fresh = []
            for n in range(states):
                value = jnp.exp2(step_now * decay_rows[n]) * carry[n] + drive_now * in_ref[base + n]
                fresh.append(value)
                if with_output:
                    part = out_ref[base + n] * value
                    total = part if total is None else total + part
            if with_output:
                y_ref[t] = total
            return tuple(fresh)

        start = tuple(init_ref[n] for n in range(states))
        final = lax.fori_loop(0, tok_count, turn, start, unroll=8)
        for n in range(states):
            end_ref[n] = final[n]

    return body


def local_scan(start_state, step3, drive3, input_map, output_map, decay3, with_output, first, count):
    tok_count, rows, lanes = step3.shape
    states = decay3.shape[0]
    blk = 8
    grid_len = count // blk
    lead = first // blk
    smem = pl.BlockSpec(memory_space=pltpu.SMEM)
    seq_spec = pl.BlockSpec((tok_count, blk, lanes), lambda j: (0, j + lead, 0))
    st_spec = pl.BlockSpec((states, blk, lanes), lambda j: (0, j + lead, 0))
    own_seq = pl.BlockSpec((tok_count, blk, lanes), lambda j: (0, j, 0))
    own_st = pl.BlockSpec((states, blk, lanes), lambda j: (0, j, 0))
    out_shape = [jax.ShapeDtypeStruct((states, count, lanes), jnp.float32)]
    out_specs = [own_st]
    if with_output:
        out_shape.insert(0, jax.ShapeDtypeStruct((tok_count, count, lanes), jnp.float32))
        out_specs.insert(0, own_seq)
    results = pl.pallas_call(
        scan_kernel(with_output),
        grid=(grid_len,),
        in_specs=[smem, smem, seq_spec, seq_spec, st_spec, own_st],
        out_specs=out_specs,
        out_shape=out_shape,
    )(input_map.reshape(-1), output_map.reshape(-1), step3, drive3, decay3, start_state)
    if with_output:
        return (results[0], results[-1])
    return (None, results[-1])


def per_device(
    tokens,
    norm_gain,
    conv_weight,
    conv_bias,
    proj_weight,
    dt_weight,
    dt_bias,
    decay_rate,
    skip_gain,
    ffn_gain,
    expert_ids,
    route_weights,
    w_gate,
    w_up,
    w_down,
):
    stream = tokens[0].astype(jnp.float32)
    tok_count = stream.shape[0]
    model_width = stream.shape[1]
    kernel = conv_weight.shape[0]
    low_width = dt_weight.shape[0]
    states = decay_rate.shape[0]
    normed = rms_scale(stream, norm_gain).astype(jnp.bfloat16)
    prior_rows = from_behind(normed[tok_count - (kernel - 1) :], "seq", 1)
    padded = jnp.concatenate([prior_rows, normed], axis=0).astype(jnp.float32)
    conv_sum = jnp.zeros((tok_count, model_width), jnp.float32)
    for offset in range(kernel):
        conv_sum = conv_sum + conv_weight[offset] * padded[offset : offset + tok_count]
    conv_out = jax.nn.silu(conv_sum + conv_bias).astype(jnp.bfloat16)
    projected = jnp.dot(conv_out, proj_weight, preferred_element_type=jnp.float32)
    low_rank = projected[:, :low_width].astype(jnp.bfloat16)
    step_size = jax.nn.softplus(
        jnp.dot(low_rank, dt_weight, preferred_element_type=jnp.float32) + dt_bias
    )
    input_map = projected[:, low_width : low_width + states]
    output_map = projected[:, low_width + states :]
    decay_neg = -decay_rate
    conv_float = conv_out.astype(jnp.float32)
    lanes = 128
    rows = model_width // lanes
    chunks = 2
    count = rows // chunks
    drive = step_size * conv_float
    step3 = step_size.reshape(tok_count, rows, lanes)
    drive3 = drive.reshape(tok_count, rows, lanes)
    decay3 = (decay_neg * math.log2(math.e)).reshape(states, rows, lanes)
    span3 = jnp.exp(decay_neg * jnp.sum(step_size, axis=0)[None, :]).reshape(states, rows, lanes)
    zero_state = jnp.zeros((states, count, lanes), jnp.float32)
    peers = lax.axis_size("seq")
    inflow = []
    for c in range(chunks):
        _, end_state = local_scan(
            zero_state, step3, drive3, input_map, output_map, decay3, False, c * count, count
        )
        summary = jnp.stack([span3[:, c * count : (c + 1) * count], end_state])
        inflow.append([from_behind(summary, "seq", k) for k in range(peers - 1, 0, -1)])
    pieces = []
    for c in range(chunks):
        incoming = jnp.zeros_like(zero_state)
        for piece in inflow[c]:
            incoming = piece[0] * incoming + piece[1]
        part, _ = local_scan(
            incoming, step3, drive3, input_map, output_map, decay3, True, c * count, count
        )
        pieces.append(part)
    scanned = jnp.concatenate(pieces, axis=1).reshape(tok_count, model_width)
    hidden_state = stream + (scanned + skip_gain * conv_float)
    ffn_in = rms_scale(hidden_state, ffn_gain).astype(jnp.bfloat16)
    owners = lax.axis_size("expert")
    experts = owners * w_gate.shape[0]
    capacity = 4 * tok_count // owners
    chosen = expert_ids[0].reshape(-1)
    onehot = (chosen[:, None] == jnp.arange(experts, dtype=jnp.int32)[None, :]).astype(jnp.int32)
    before = jnp.cumsum(onehot, axis=0) - onehot
    slot_pos = jnp.sum(before * onehot, axis=1)
    dest_row = chosen * capacity + slot_pos
    slot_ids = jnp.arange(experts * capacity, dtype=jnp.int32)
    pair_rows = dest_row.reshape(tok_count, 2)
    place_map = (
        (slot_ids[:, None] == pair_rows[None, :, 0]) | (slot_ids[:, None] == pair_rows[None, :, 1])
    ).astype(jnp.bfloat16)
    outgoing = jnp.dot(place_map, ffn_in, preferred_element_type=jnp.float32).astype(jnp.bfloat16)
    outgoing = outgoing.reshape(experts, capacity, model_width)
    received = lax.all_to_all(outgoing, "expert", split_axis=0, concat_axis=0, tiled=True)
    recv_shape = received.shape
    rows_in = received.reshape(-1, model_width)
    gate_part = jnp.dot(rows_in, w_gate[0], preferred_element_type=jnp.float32)
    up_part = jnp.dot(rows_in, w_up[0], preferred_element_type=jnp.float32)
    inner_act = (jax.nn.silu(gate_part) * up_part).astype(jnp.bfloat16)
    result = jnp.dot(inner_act, w_down[0], preferred_element_type=jnp.float32).astype(jnp.bfloat16)
    returned = lax.all_to_all(
        result.reshape(recv_shape), "expert", split_axis=0, concat_axis=0, tiled=True
    )
    flat_back = returned.reshape(experts * capacity, model_width)
    picks = [
        jnp.dot(
            (pair_rows[:, k][:, None] == slot_ids[None, :]).astype(jnp.bfloat16),
            flat_back,
            preferred_element_type=jnp.bfloat16,
        ).astype(jnp.float32)
        for k in range(2)
    ]
    route_scale = route_weights[0]
    routed = route_scale[:, 0:1] * picks[0] + route_scale[:, 1:2] * picks[1]
    block_out = (hidden_state + routed).astype(jnp.bfloat16)
    return block_out[None]


def solution(mesh):
    in_specs = (
        P("expert", "seq", None),
        P(),
        P(),
        P(),
        P(),
        P(),
        P(),
        P(),
        P(),
        P(),
        P("expert", "seq", None),
        P("expert", "seq", None),
        P("expert", None, None),
        P("expert", None, None),
        P("expert", None, None),
    )
    out_specs = P("expert", "seq", None)
    return jax.shard_map(
        per_device, mesh=mesh, in_specs=in_specs, out_specs=out_specs, check_vma=False
    )
```

```python
import math

import jax
import jax.numpy as jnp
from jax import lax
from jax.sharding import PartitionSpec as P
from jax.experimental import pallas as pl
from jax.experimental.pallas import tpu as pltpu


def from_behind(array, axis, by):
    peers = lax.axis_size(axis)
    pairs = [(i, i + by) for i in range(peers) if 0 <= i + by < peers]
    return lax.ppermute(array, axis, pairs)


def prefix(array, axis, combine, identity):
    peers, place = (lax.axis_size(axis), lax.axis_index(axis))
    everything = jax.tree.map(lambda part: lax.all_gather(part, axis), array)
    start = jax.tree.map(
        lambda part, zero: jnp.broadcast_to(jnp.asarray(zero, part.dtype), part.shape),
        array,
        identity,
    )

    def turn(k, before):
        reached = k < place
        new = combine(before, jax.tree.map(lambda part: part[k], everything))
        return jax.tree.map(lambda a, b: jnp.where(reached, a, b), new, before)

    return lax.fori_loop(0, peers, turn, start)


def rms_scale(values, gain):
    return values * lax.rsqrt(jnp.mean(values * values, axis=-1, keepdims=True) + 1e-05) * gain


def scan_kernel(with_output):
    def body(in_ref, out_ref, step_ref, drive_ref, decay_ref, init_ref, *outs):
        states = decay_ref.shape[0]
        tok_count = step_ref.shape[0]
        decay_rows = [decay_ref[n] for n in range(states)]
        if with_output:
            y_ref, end_ref = outs
        else:
            (end_ref,) = outs

        def turn(t, carry):
            step_now = step_ref[t]
            drive_now = drive_ref[t]
            base = t * states
            total = None
            fresh = []
            for n in range(states):
                value = jnp.exp2(step_now * decay_rows[n]) * carry[n] + drive_now * in_ref[base + n]
                fresh.append(value)
                if with_output:
                    part = out_ref[base + n] * value
                    total = part if total is None else total + part
            if with_output:
                y_ref[t] = total
            return tuple(fresh)

        start = tuple(init_ref[n] for n in range(states))
        final = lax.fori_loop(0, tok_count, turn, start, unroll=8)
        for n in range(states):
            end_ref[n] = final[n]

    return body


def local_scan(start_state, step3, drive3, input_map, output_map, decay3, with_output, first, count):
    tok_count, rows, lanes = step3.shape
    states = decay3.shape[0]
    blk = 8
    grid_len = count // blk
    lead = first // blk
    smem = pl.BlockSpec(memory_space=pltpu.SMEM)
    seq_spec = pl.BlockSpec((tok_count, blk, lanes), lambda j: (0, j + lead, 0))
    st_spec = pl.BlockSpec((states, blk, lanes), lambda j: (0, j + lead, 0))
    own_seq = pl.BlockSpec((tok_count, blk, lanes), lambda j: (0, j, 0))
    own_st = pl.BlockSpec((states, blk, lanes), lambda j: (0, j, 0))
    out_shape = [jax.ShapeDtypeStruct((states, count, lanes), jnp.float32)]
    out_specs = [own_st]
    if with_output:
        out_shape.insert(0, jax.ShapeDtypeStruct((tok_count, count, lanes), jnp.float32))
        out_specs.insert(0, own_seq)
    results = pl.pallas_call(
        scan_kernel(with_output),
        grid=(grid_len,),
        in_specs=[smem, smem, seq_spec, seq_spec, st_spec, own_st],
        out_specs=out_specs,
        out_shape=out_shape,
    )(input_map.reshape(-1), output_map.reshape(-1), step3, drive3, decay3, start_state)
    if with_output:
        return (results[0], results[-1])
    return (None, results[-1])


def per_device(
    tokens,
    norm_gain,
    conv_weight,
    conv_bias,
    proj_weight,
    dt_weight,
    dt_bias,
    decay_rate,
    skip_gain,
    ffn_gain,
    expert_ids,
    route_weights,
    w_gate,
    w_up,
    w_down,
):
    stream = tokens[0].astype(jnp.float32)
    tok_count = stream.shape[0]
    model_width = stream.shape[1]
    kernel = conv_weight.shape[0]
    low_width = dt_weight.shape[0]
    states = decay_rate.shape[0]
    normed = rms_scale(stream, norm_gain).astype(jnp.bfloat16)
    prior_rows = from_behind(normed[tok_count - (kernel - 1) :], "seq", 1)
    padded = jnp.concatenate([prior_rows, normed], axis=0).astype(jnp.float32)
    conv_sum = jnp.zeros((tok_count, model_width), jnp.float32)
    for offset in range(kernel):
        conv_sum = conv_sum + conv_weight[offset] * padded[offset : offset + tok_count]
    conv_out = jax.nn.silu(conv_sum + conv_bias).astype(jnp.bfloat16)
    projected = jnp.dot(conv_out, proj_weight, preferred_element_type=jnp.float32)
    low_rank = projected[:, :low_width].astype(jnp.bfloat16)
    step_size = jax.nn.softplus(
        jnp.dot(low_rank, dt_weight, preferred_element_type=jnp.float32) + dt_bias
    )
    input_map = projected[:, low_width : low_width + states]
    output_map = projected[:, low_width + states :]
    decay_neg = -decay_rate
    conv_float = conv_out.astype(jnp.float32)
    lanes = 128
    rows = model_width // lanes
    chunks = 2
    count = rows // chunks
    drive = step_size * conv_float
    step3 = step_size.reshape(tok_count, rows, lanes)
    drive3 = drive.reshape(tok_count, rows, lanes)
    decay3 = (decay_neg * math.log2(math.e)).reshape(states, rows, lanes)
    span3 = jnp.exp(decay_neg * jnp.sum(step_size, axis=0)[None, :]).reshape(states, rows, lanes)
    zero_state = jnp.zeros((states, count, lanes), jnp.float32)
    inflow = []
    for c in range(chunks):
        _, end_state = local_scan(
            zero_state, step3, drive3, input_map, output_map, decay3, False, c * count, count
        )
        own_decay = span3[:, c * count : (c + 1) * count]
        near = from_behind(jnp.stack([own_decay, end_state]), "seq", 1)
        paired = own_decay * near[1] + end_state
        inflow.append((near, from_behind(paired, "seq", 2)))
    pieces = []
    for c in range(chunks):
        near, far = inflow[c]
        incoming = near[0] * far + near[1]
        part, _ = local_scan(
            incoming, step3, drive3, input_map, output_map, decay3, True, c * count, count
        )
        pieces.append(part)
    scanned = jnp.concatenate(pieces, axis=1).reshape(tok_count, model_width)
    hidden_state = stream + (scanned + skip_gain * conv_float)
    ffn_in = rms_scale(hidden_state, ffn_gain).astype(jnp.bfloat16)
    owners = lax.axis_size("expert")
    experts = owners * w_gate.shape[0]
    capacity = 4 * tok_count // owners
    chosen = expert_ids[0].reshape(-1)
    onehot = (chosen[:, None] == jnp.arange(experts, dtype=jnp.int32)[None, :]).astype(jnp.int32)
    before = jnp.cumsum(onehot, axis=0) - onehot
    slot_pos = jnp.sum(before * onehot, axis=1)
    dest_row = chosen * capacity + slot_pos
    slot_ids = jnp.arange(experts * capacity, dtype=jnp.int32)
    pair_rows = dest_row.reshape(tok_count, 2)
    place_map = (
        (slot_ids[:, None] == pair_rows[None, :, 0]) | (slot_ids[:, None] == pair_rows[None, :, 1])
    ).astype(jnp.bfloat16)
    outgoing = jnp.dot(place_map, ffn_in, preferred_element_type=jnp.float32).astype(jnp.bfloat16)
    outgoing = outgoing.reshape(experts, capacity, model_width)
    received = lax.all_to_all(outgoing, "expert", split_axis=0, concat_axis=0, tiled=True)
    recv_shape = received.shape
    rows_in = received.reshape(-1, model_width)
    gate_part = jnp.dot(rows_in, w_gate[0], preferred_element_type=jnp.float32)
    up_part = jnp.dot(rows_in, w_up[0], preferred_element_type=jnp.float32)
    inner_act = (jax.nn.silu(gate_part) * up_part).astype(jnp.bfloat16)
    result = jnp.dot(inner_act, w_down[0], preferred_element_type=jnp.float32).astype(jnp.bfloat16)
    returned = lax.all_to_all(
        result.reshape(recv_shape), "expert", split_axis=0, concat_axis=0, tiled=True
    )
    flat_back = returned.reshape(experts * capacity, model_width)
    picks = [
        jnp.dot(
            (pair_rows[:, k][:, None] == slot_ids[None, :]).astype(jnp.bfloat16),
            flat_back,
            preferred_element_type=jnp.bfloat16,
        ).astype(jnp.float32)
        for k in range(2)
    ]
    route_scale = route_weights[0]
    routed = route_scale[:, 0:1] * picks[0] + route_scale[:, 1:2] * picks[1]
    block_out = (hidden_state + routed).astype(jnp.bfloat16)
    return block_out[None]


def solution(mesh):
    in_specs = (
        P("expert", "seq", None),
        P(),
        P(),
        P(),
        P(),
        P(),
        P(),
        P(),
        P(),
        P(),
        P("expert", "seq", None),
        P("expert", "seq", None),
        P("expert", None, None),
        P("expert", None, None),
        P("expert", None, None),
    )
    out_specs = P("expert", "seq", None)
    return jax.shard_map(
        per_device, mesh=mesh, in_specs=in_specs, out_specs=out_specs, check_vma=False
    )
```

```python
import math

import jax
import jax.numpy as jnp
from jax import lax
from jax.sharding import PartitionSpec as P
from jax.experimental import pallas as pl
from jax.experimental.pallas import tpu as pltpu


def from_behind(array, axis, by):
    peers = lax.axis_size(axis)
    pairs = [(i, i + by) for i in range(peers) if 0 <= i + by < peers]
    return lax.ppermute(array, axis, pairs)


def prefix(array, axis, combine, identity):
    peers, place = (lax.axis_size(axis), lax.axis_index(axis))
    everything = jax.tree.map(lambda part: lax.all_gather(part, axis), array)
    start = jax.tree.map(
        lambda part, zero: jnp.broadcast_to(jnp.asarray(zero, part.dtype), part.shape),
        array,
        identity,
    )

    def turn(k, before):
        reached = k < place
        new = combine(before, jax.tree.map(lambda part: part[k], everything))
        return jax.tree.map(lambda a, b: jnp.where(reached, a, b), new, before)

    return lax.fori_loop(0, peers, turn, start)


def rms_scale(values, gain):
    return values * lax.rsqrt(jnp.mean(values * values, axis=-1, keepdims=True) + 1e-05) * gain


def scan_kernel(with_output):
    def body(in_ref, out_ref, step_ref, drive_ref, decay_ref, init_ref, *outs):
        states = decay_ref.shape[0]
        tok_count = step_ref.shape[0]
        decay_rows = [decay_ref[n] for n in range(states)]
        if with_output:
            y_ref, end_ref = outs
        else:
            (end_ref,) = outs

        def turn(t, carry):
            step_now = step_ref[t]
            drive_now = drive_ref[t]
            base = t * states
            total = None
            fresh = []
            for n in range(states):
                value = jnp.exp2(step_now * decay_rows[n]) * carry[n] + drive_now * in_ref[base + n]
                fresh.append(value)
                if with_output:
                    part = out_ref[base + n] * value
                    total = part if total is None else total + part
            if with_output:
                y_ref[t] = total
            return tuple(fresh)

        start = tuple(init_ref[n] for n in range(states))
        final = lax.fori_loop(0, tok_count, turn, start, unroll=8)
        for n in range(states):
            end_ref[n] = final[n]

    return body


def local_scan(start_state, step3, drive3, input_map, output_map, decay3, with_output, first, count):
    tok_count, rows, lanes = step3.shape
    states = decay3.shape[0]
    blk = 8
    grid_len = count // blk
    lead = first // blk
    smem = pl.BlockSpec(memory_space=pltpu.SMEM)
    seq_spec = pl.BlockSpec((tok_count, blk, lanes), lambda j: (0, j + lead, 0))
    st_spec = pl.BlockSpec((states, blk, lanes), lambda j: (0, j + lead, 0))
    own_seq = pl.BlockSpec((tok_count, blk, lanes), lambda j: (0, j, 0))
    own_st = pl.BlockSpec((states, blk, lanes), lambda j: (0, j, 0))
    out_shape = [jax.ShapeDtypeStruct((states, count, lanes), jnp.float32)]
    out_specs = [own_st]
    if with_output:
        out_shape.insert(0, jax.ShapeDtypeStruct((tok_count, count, lanes), jnp.float32))
        out_specs.insert(0, own_seq)
    results = pl.pallas_call(
        scan_kernel(with_output),
        grid=(grid_len,),
        in_specs=[smem, smem, seq_spec, seq_spec, st_spec, own_st],
        out_specs=out_specs,
        out_shape=out_shape,
    )(input_map.reshape(-1), output_map.reshape(-1), step3, drive3, decay3, start_state)
    if with_output:
        return (results[0], results[-1])
    return (None, results[-1])


def per_device(
    tokens,
    norm_gain,
    conv_weight,
    conv_bias,
    proj_weight,
    dt_weight,
    dt_bias,
    decay_rate,
    skip_gain,
    ffn_gain,
    expert_ids,
    route_weights,
    w_gate,
    w_up,
    w_down,
):
    stream = tokens[0].astype(jnp.float32)
    tok_count = stream.shape[0]
    model_width = stream.shape[1]
    kernel = conv_weight.shape[0]
    low_width = dt_weight.shape[0]
    states = decay_rate.shape[0]
    normed = rms_scale(stream, norm_gain).astype(jnp.bfloat16)
    prior_rows = from_behind(normed[tok_count - (kernel - 1) :], "seq", 1)
    padded = jnp.concatenate([prior_rows, normed], axis=0).astype(jnp.float32)
    conv_sum = jnp.zeros((tok_count, model_width), jnp.float32)
    for offset in range(kernel):
        conv_sum = conv_sum + conv_weight[offset] * padded[offset : offset + tok_count]
    conv_out = jax.nn.silu(conv_sum + conv_bias).astype(jnp.bfloat16)
    projected = jnp.dot(conv_out, proj_weight, preferred_element_type=jnp.float32)
    low_rank = projected[:, :low_width].astype(jnp.bfloat16)
    step_size = jax.nn.softplus(
        jnp.dot(low_rank, dt_weight, preferred_element_type=jnp.float32) + dt_bias
    )
    input_map = projected[:, low_width : low_width + states]
    output_map = projected[:, low_width + states :]
    decay_neg = -decay_rate
    conv_float = conv_out.astype(jnp.float32)
    lanes = 128
    rows = model_width // lanes
    chunks = 2
    count = rows // chunks
    drive = step_size * conv_float
    step3 = step_size.reshape(tok_count, rows, lanes)
    drive3 = drive.reshape(tok_count, rows, lanes)
    decay3 = (decay_neg * math.log2(math.e)).reshape(states, rows, lanes)
    span3 = jnp.exp(decay_neg * jnp.sum(step_size, axis=0)[None, :]).reshape(states, rows, lanes)
    zero_state = jnp.zeros((states, count, lanes), jnp.float32)
    peers = lax.axis_size("seq")
    inflow = []
    for c in range(chunks):
        _, end_state = local_scan(
            zero_state, step3, drive3, input_map, output_map, decay3, False, c * count, count
        )
        summary = jnp.stack([span3[:, c * count : (c + 1) * count], end_state])
        inflow.append([from_behind(summary, "seq", k) for k in range(peers - 1, 0, -1)])
    pieces = []
    for c in range(chunks):
        incoming = jnp.zeros_like(zero_state)
        for piece in inflow[c]:
            incoming = piece[0] * incoming + piece[1]
        part, _ = local_scan(
            incoming, step3, drive3, input_map, output_map, decay3, True, c * count, count
        )
        pieces.append(part)
    scanned = jnp.concatenate(pieces, axis=1).reshape(tok_count, model_width)
    hidden_state = stream + (scanned + skip_gain * conv_float)
    ffn_in = rms_scale(hidden_state, ffn_gain).astype(jnp.bfloat16)
    owners = lax.axis_size("expert")
    experts = owners * w_gate.shape[0]
    capacity = 4 * tok_count // owners
    chosen = expert_ids[0].reshape(-1)
    onehot = (chosen[:, None] == jnp.arange(experts, dtype=jnp.int32)[None, :]).astype(jnp.bfloat16)
    pair_ids = jnp.arange(chosen.shape[0], dtype=jnp.int32)
    earlier = (pair_ids[:, None] > pair_ids[None, :]).astype(jnp.bfloat16)
    before = jnp.dot(earlier, onehot, preferred_element_type=jnp.float32)
    slot_pos = jnp.sum(before * onehot.astype(jnp.float32), axis=1).astype(jnp.int32)
    dest_row = chosen * capacity + slot_pos
    slot_ids = jnp.arange(experts * capacity, dtype=jnp.int32)
    pair_rows = dest_row.reshape(tok_count, 2)
    place_map = (
        (slot_ids[:, None] == pair_rows[None, :, 0]) | (slot_ids[:, None] == pair_rows[None, :, 1])
    ).astype(jnp.bfloat16)
    outgoing = jnp.dot(place_map, ffn_in, preferred_element_type=jnp.float32).astype(jnp.bfloat16)
    outgoing = outgoing.reshape(experts, capacity, model_width)
    received = lax.all_to_all(outgoing, "expert", split_axis=0, concat_axis=0, tiled=True)
    recv_shape = received.shape
    rows_in = received.reshape(-1, model_width)
    gate_part = jnp.dot(rows_in, w_gate[0], preferred_element_type=jnp.float32)
    up_part = jnp.dot(rows_in, w_up[0], preferred_element_type=jnp.float32)
    inner_act = (jax.nn.silu(gate_part) * up_part).astype(jnp.bfloat16)
    result = jnp.dot(inner_act, w_down[0], preferred_element_type=jnp.float32).astype(jnp.bfloat16)
    returned = lax.all_to_all(
        result.reshape(recv_shape), "expert", split_axis=0, concat_axis=0, tiled=True
    )
    flat_back = returned.reshape(experts * capacity, model_width)
    picks = [
        jnp.dot(
            (pair_rows[:, k][:, None] == slot_ids[None, :]).astype(jnp.bfloat16),
            flat_back,
            preferred_element_type=jnp.bfloat16,
        ).astype(jnp.float32)
        for k in range(2)
    ]
    route_scale = route_weights[0]
    routed = route_scale[:, 0:1] * picks[0] + route_scale[:, 1:2] * picks[1]
    block_out = (hidden_state + routed).astype(jnp.bfloat16)
    return block_out[None]


def solution(mesh):
    in_specs = (
        P("expert", "seq", None),
        P(),
        P(),
        P(),
        P(),
        P(),
        P(),
        P(),
        P(),
        P(),
        P("expert", "seq", None),
        P("expert", "seq", None),
        P("expert", None, None),
        P("expert", None, None),
        P("expert", None, None),
    )
    out_specs = P("expert", "seq", None)
    return jax.shard_map(
        per_device, mesh=mesh, in_specs=in_specs, out_specs=out_specs, check_vma=False
    )
```

```python
import math

import jax
import jax.numpy as jnp
from jax import lax
from jax.sharding import PartitionSpec as P
from jax.experimental import pallas as pl
from jax.experimental.pallas import tpu as pltpu


def from_behind(array, axis, by):
    peers = lax.axis_size(axis)
    pairs = [(i, i + by) for i in range(peers) if 0 <= i + by < peers]
    return lax.ppermute(array, axis, pairs)


def prefix(array, axis, combine, identity):
    peers, place = (lax.axis_size(axis), lax.axis_index(axis))
    everything = jax.tree.map(lambda part: lax.all_gather(part, axis), array)
    start = jax.tree.map(
        lambda part, zero: jnp.broadcast_to(jnp.asarray(zero, part.dtype), part.shape),
        array,
        identity,
    )

    def turn(k, before):
        reached = k < place
        new = combine(before, jax.tree.map(lambda part: part[k], everything))
        return jax.tree.map(lambda a, b: jnp.where(reached, a, b), new, before)

    return lax.fori_loop(0, peers, turn, start)


def rms_scale(values, gain):
    return values * lax.rsqrt(jnp.mean(values * values, axis=-1, keepdims=True) + 1e-05) * gain


def scan_kernel(with_output):
    def body(in_ref, out_ref, step_ref, drive_ref, decay_ref, init_ref, *outs):
        states = decay_ref.shape[0]
        tok_count = step_ref.shape[0]
        decay_rows = [decay_ref[n] for n in range(states)]
        if with_output:
            y_ref, end_ref = outs
        else:
            (end_ref,) = outs

        def turn(t, carry):
            step_now = step_ref[t]
            drive_now = step_now * drive_ref[t].astype(jnp.float32)
            base = t * states
            total = None
            fresh = []
            for n in range(states):
                value = jnp.exp2(step_now * decay_rows[n]) * carry[n] + drive_now * in_ref[base + n]
                fresh.append(value)
                if with_output:
                    part = out_ref[base + n] * value
                    total = part if total is None else total + part
            if with_output:
                y_ref[t] = total
            return tuple(fresh)

        start = tuple(init_ref[n] for n in range(states))
        final = lax.fori_loop(0, tok_count, turn, start, unroll=8)
        for n in range(states):
            end_ref[n] = final[n]

    return body


def local_scan(start_state, step3, drive3, input_map, output_map, decay3, with_output, first, count):
    tok_count, rows, lanes = step3.shape
    states = decay3.shape[0]
    blk = 8
    grid_len = count // blk
    lead = first // blk
    smem = pl.BlockSpec(memory_space=pltpu.SMEM)
    seq_spec = pl.BlockSpec((tok_count, blk, lanes), lambda j: (0, j + lead, 0))
    st_spec = pl.BlockSpec((states, blk, lanes), lambda j: (0, j + lead, 0))
    own_seq = pl.BlockSpec((tok_count, blk, lanes), lambda j: (0, j, 0))
    own_st = pl.BlockSpec((states, blk, lanes), lambda j: (0, j, 0))
    out_shape = [jax.ShapeDtypeStruct((states, count, lanes), jnp.float32)]
    out_specs = [own_st]
    if with_output:
        out_shape.insert(0, jax.ShapeDtypeStruct((tok_count, count, lanes), jnp.float32))
        out_specs.insert(0, own_seq)
    results = pl.pallas_call(
        scan_kernel(with_output),
        grid=(grid_len,),
        in_specs=[smem, smem, seq_spec, seq_spec, st_spec, own_st],
        out_specs=out_specs,
        out_shape=out_shape,
    )(input_map.reshape(-1), output_map.reshape(-1), step3, drive3, decay3, start_state)
    if with_output:
        return (results[0], results[-1])
    return (None, results[-1])


def per_device(
    tokens,
    norm_gain,
    conv_weight,
    conv_bias,
    proj_weight,
    dt_weight,
    dt_bias,
    decay_rate,
    skip_gain,
    ffn_gain,
    expert_ids,
    route_weights,
    w_gate,
    w_up,
    w_down,
):
    stream = tokens[0].astype(jnp.float32)
    tok_count = stream.shape[0]
    model_width = stream.shape[1]
    kernel = conv_weight.shape[0]
    low_width = dt_weight.shape[0]
    states = decay_rate.shape[0]
    normed = rms_scale(stream, norm_gain).astype(jnp.bfloat16)
    prior_rows = from_behind(normed[tok_count - (kernel - 1) :], "seq", 1)
    padded = jnp.concatenate([prior_rows, normed], axis=0).astype(jnp.float32)
    conv_sum = jnp.zeros((tok_count, model_width), jnp.float32)
    for offset in range(kernel):
        conv_sum = conv_sum + conv_weight[offset] * padded[offset : offset + tok_count]
    conv_out = jax.nn.silu(conv_sum + conv_bias).astype(jnp.bfloat16)
    projected = jnp.dot(conv_out, proj_weight, preferred_element_type=jnp.float32)
    low_rank = projected[:, :low_width].astype(jnp.bfloat16)
    step_size = jax.nn.softplus(
        jnp.dot(low_rank, dt_weight, preferred_element_type=jnp.float32) + dt_bias
    )
    input_map = projected[:, low_width : low_width + states]
    output_map = projected[:, low_width + states :]
    decay_neg = -decay_rate
    conv_float = conv_out.astype(jnp.float32)
    lanes = 128
    rows = model_width // lanes
    chunks = 2
    count = rows // chunks
    step3 = step_size.reshape(tok_count, rows, lanes)
    drive3 = conv_out.reshape(tok_count, rows, lanes)
    decay3 = (decay_neg * math.log2(math.e)).reshape(states, rows, lanes)
    span3 = jnp.exp(decay_neg * jnp.sum(step_size, axis=0)[None, :]).reshape(states, rows, lanes)
    zero_state = jnp.zeros((states, count, lanes), jnp.float32)
    peers = lax.axis_size("seq")
    inflow = []
    for c in range(chunks):
        _, end_state = local_scan(
            zero_state, step3, drive3, input_map, output_map, decay3, False, c * count, count
        )
        summary = jnp.stack([span3[:, c * count : (c + 1) * count], end_state])
        inflow.append([from_behind(summary, "seq", k) for k in range(peers - 1, 0, -1)])
    pieces = []
    for c in range(chunks):
        incoming = jnp.zeros_like(zero_state)
        for piece in inflow[c]:
            incoming = piece[0] * incoming + piece[1]
        part, _ = local_scan(
            incoming, step3, drive3, input_map, output_map, decay3, True, c * count, count
        )
        pieces.append(part)
    scanned = jnp.concatenate(pieces, axis=1).reshape(tok_count, model_width)
    hidden_state = stream + (scanned + skip_gain * conv_float)
    ffn_in = rms_scale(hidden_state, ffn_gain).astype(jnp.bfloat16)
    owners = lax.axis_size("expert")
    experts = owners * w_gate.shape[0]
    capacity = 4 * tok_count // owners
    chosen = expert_ids[0].reshape(-1)
    onehot = (chosen[:, None] == jnp.arange(experts, dtype=jnp.int32)[None, :]).astype(jnp.bfloat16)
    pair_ids = jnp.arange(chosen.shape[0], dtype=jnp.int32)
    earlier = (pair_ids[:, None] > pair_ids[None, :]).astype(jnp.bfloat16)
    before = jnp.dot(earlier, onehot, preferred_element_type=jnp.float32)
    slot_pos = jnp.sum(before * onehot.astype(jnp.float32), axis=1).astype(jnp.int32)
    dest_row = chosen * capacity + slot_pos
    slot_ids = jnp.arange(experts * capacity, dtype=jnp.int32)
    pair_rows = dest_row.reshape(tok_count, 2)
    place_map = (
        (slot_ids[:, None] == pair_rows[None, :, 0]) | (slot_ids[:, None] == pair_rows[None, :, 1])
    ).astype(jnp.bfloat16)
    outgoing = jnp.dot(place_map, ffn_in, preferred_element_type=jnp.float32).astype(jnp.bfloat16)
    outgoing = outgoing.reshape(experts, capacity, model_width)
    received = lax.all_to_all(outgoing, "expert", split_axis=0, concat_axis=0, tiled=True)
    recv_shape = received.shape
    rows_in = received.reshape(-1, model_width)
    gate_part = jnp.dot(rows_in, w_gate[0], preferred_element_type=jnp.float32)
    up_part = jnp.dot(rows_in, w_up[0], preferred_element_type=jnp.float32)
    inner_act = (jax.nn.silu(gate_part) * up_part).astype(jnp.bfloat16)
    result = jnp.dot(inner_act, w_down[0], preferred_element_type=jnp.float32).astype(jnp.bfloat16)
    returned = lax.all_to_all(
        result.reshape(recv_shape), "expert", split_axis=0, concat_axis=0, tiled=True
    )
    flat_back = returned.reshape(experts * capacity, model_width)
    picks = [
        jnp.dot(
            (pair_rows[:, k][:, None] == slot_ids[None, :]).astype(jnp.bfloat16),
            flat_back,
            preferred_element_type=jnp.bfloat16,
        ).astype(jnp.float32)
        for k in range(2)
    ]
    route_scale = route_weights[0]
    routed = route_scale[:, 0:1] * picks[0] + route_scale[:, 1:2] * picks[1]
    block_out = (hidden_state + routed).astype(jnp.bfloat16)
    return block_out[None]


def solution(mesh):
    in_specs = (
        P("expert", "seq", None),
        P(),
        P(),
        P(),
        P(),
        P(),
        P(),
        P(),
        P(),
        P(),
        P("expert", "seq", None),
        P("expert", "seq", None),
        P("expert", None, None),
        P("expert", None, None),
        P("expert", None, None),
    )
    out_specs = P("expert", "seq", None)
    return jax.shard_map(
        per_device, mesh=mesh, in_specs=in_specs, out_specs=out_specs, check_vma=False
    )
```

```python
import math

import jax
import jax.numpy as jnp
from jax import lax
from jax.sharding import PartitionSpec as P
from jax.experimental import pallas as pl
from jax.experimental.pallas import tpu as pltpu


def from_behind(array, axis, by):
    peers = lax.axis_size(axis)
    pairs = [(i, i + by) for i in range(peers) if 0 <= i + by < peers]
    return lax.ppermute(array, axis, pairs)


def prefix(array, axis, combine, identity):
    peers, place = (lax.axis_size(axis), lax.axis_index(axis))
    everything = jax.tree.map(lambda part: lax.all_gather(part, axis), array)
    start = jax.tree.map(
        lambda part, zero: jnp.broadcast_to(jnp.asarray(zero, part.dtype), part.shape),
        array,
        identity,
    )

    def turn(k, before):
        reached = k < place
        new = combine(before, jax.tree.map(lambda part: part[k], everything))
        return jax.tree.map(lambda a, b: jnp.where(reached, a, b), new, before)

    return lax.fori_loop(0, peers, turn, start)


def rms_scale(values, gain):
    return values * lax.rsqrt(jnp.mean(values * values, axis=-1, keepdims=True) + 1e-05) * gain


def scan_kernel(with_output):
    def body(in_ref, out_ref, step_ref, drive_ref, decay_ref, init_ref, *outs):
        states = decay_ref.shape[0]
        tok_count = step_ref.shape[0]
        decay_rows = [decay_ref[n] for n in range(states)]
        if with_output:
            y_ref, end_ref = outs
        else:
            (end_ref,) = outs

        def turn(t, carry):
            step_now = step_ref[t]
            drive_now = step_now * drive_ref[t].astype(jnp.float32)
            base = t * states
            total = None
            fresh = []
            for n in range(states):
                value = jnp.exp2(step_now * decay_rows[n]) * carry[n] + drive_now * in_ref[base + n]
                fresh.append(value)
                if with_output:
                    part = out_ref[base + n] * value
                    total = part if total is None else total + part
            if with_output:
                y_ref[t] = total
            return tuple(fresh)

        if with_output:
            start = tuple(init_ref[n] for n in range(states))
        else:
            start = tuple(jnp.zeros(decay_rows[0].shape, jnp.float32) for n in range(states))
        final = lax.fori_loop(0, tok_count, turn, start, unroll=8)
        for n in range(states):
            end_ref[n] = final[n]

    return body


def local_scan(start_state, step3, drive3, input_map, output_map, decay3, with_output, first, count):
    tok_count, rows, lanes = step3.shape
    states = decay3.shape[0]
    blk = 8
    grid_len = count // blk
    lead = first // blk
    smem = pl.BlockSpec(memory_space=pltpu.SMEM)
    seq_spec = pl.BlockSpec((tok_count, blk, lanes), lambda j: (0, j + lead, 0))
    st_spec = pl.BlockSpec((states, blk, lanes), lambda j: (0, j + lead, 0))
    own_seq = pl.BlockSpec((tok_count, blk, lanes), lambda j: (0, j, 0))
    own_st = pl.BlockSpec((states, blk, lanes), lambda j: (0, j, 0))
    out_shape = [jax.ShapeDtypeStruct((states, count, lanes), jnp.float32)]
    out_specs = [own_st]
    if with_output:
        out_shape.insert(0, jax.ShapeDtypeStruct((tok_count, count, lanes), jnp.float32))
        out_specs.insert(0, own_seq)
    operands = [input_map.reshape(-1), output_map.reshape(-1), step3, drive3, decay3]
    in_specs = [smem, smem, seq_spec, seq_spec, st_spec]
    body = scan_kernel(with_output)
    if with_output:
        operands.append(start_state)
        in_specs.append(own_st)
    else:
        plain = body
        body = lambda a, b, c, d, e, *outs: plain(a, b, c, d, e, None, *outs)
    results = pl.pallas_call(
        body,
        grid=(grid_len,),
        in_specs=in_specs,
        out_specs=out_specs,
        out_shape=out_shape,
    )(*operands)
    if with_output:
        return (results[0], results[-1])
    return (None, results[-1])


def per_device(
    tokens,
    norm_gain,
    conv_weight,
    conv_bias,
    proj_weight,
    dt_weight,
    dt_bias,
    decay_rate,
    skip_gain,
    ffn_gain,
    expert_ids,
    route_weights,
    w_gate,
    w_up,
    w_down,
):
    stream = tokens[0].astype(jnp.float32)
    tok_count = stream.shape[0]
    model_width = stream.shape[1]
    kernel = conv_weight.shape[0]
    low_width = dt_weight.shape[0]
    states = decay_rate.shape[0]
    normed = rms_scale(stream, norm_gain).astype(jnp.bfloat16)
    prior_rows = from_behind(normed[tok_count - (kernel - 1) :], "seq", 1)
    padded = jnp.concatenate([prior_rows, normed], axis=0).astype(jnp.float32)
    conv_sum = jnp.zeros((tok_count, model_width), jnp.float32)
    for offset in range(kernel):
        conv_sum = conv_sum + conv_weight[offset] * padded[offset : offset + tok_count]
    conv_out = jax.nn.silu(conv_sum + conv_bias).astype(jnp.bfloat16)
    projected = jnp.dot(conv_out, proj_weight, preferred_element_type=jnp.float32)
    low_rank = projected[:, :low_width].astype(jnp.bfloat16)
    step_size = jax.nn.softplus(
        jnp.dot(low_rank, dt_weight, preferred_element_type=jnp.float32) + dt_bias
    )
    input_map = projected[:, low_width : low_width + states]
    output_map = projected[:, low_width + states :]
    decay_neg = -decay_rate
    conv_float = conv_out.astype(jnp.float32)
    lanes = 128
    rows = model_width // lanes
    chunks = 2
    count = rows // chunks
    step3 = step_size.reshape(tok_count, rows, lanes)
    drive3 = conv_out.reshape(tok_count, rows, lanes)
    decay3 = (decay_neg * math.log2(math.e)).reshape(states, rows, lanes)
    span3 = jnp.exp(decay_neg * jnp.sum(step_size, axis=0)[None, :]).reshape(states, rows, lanes)
    zero_state = jnp.zeros((states, count, lanes), jnp.float32)
    peers = lax.axis_size("seq")
    inflow = []
    for c in range(chunks):
        _, end_state = local_scan(
            None, step3, drive3, input_map, output_map, decay3, False, c * count, count
        )
        summary = jnp.stack([span3[:, c * count : (c + 1) * count], end_state])
        inflow.append([from_behind(summary, "seq", k) for k in range(peers - 1, 0, -1)])
    pieces = []
    for c in range(chunks):
        incoming = jnp.zeros_like(zero_state)
        for piece in inflow[c]:
            incoming = piece[0] * incoming + piece[1]
        part, _ = local_scan(
            incoming, step3, drive3, input_map, output_map, decay3, True, c * count, count
        )
        pieces.append(part)
    scanned = jnp.concatenate(pieces, axis=1).reshape(tok_count, model_width)
    hidden_state = stream + (scanned + skip_gain * conv_float)
    ffn_in = rms_scale(hidden_state, ffn_gain).astype(jnp.bfloat16)
    owners = lax.axis_size("expert")
    experts = owners * w_gate.shape[0]
    capacity = 4 * tok_count // owners
    chosen = expert_ids[0].reshape(-1)
    onehot = (chosen[:, None] == jnp.arange(experts, dtype=jnp.int32)[None, :]).astype(jnp.bfloat16)
    pair_ids = jnp.arange(chosen.shape[0], dtype=jnp.int32)
    earlier = (pair_ids[:, None] > pair_ids[None, :]).astype(jnp.bfloat16)
    before = jnp.dot(earlier, onehot, preferred_element_type=jnp.float32)
    slot_pos = jnp.sum(before * onehot.astype(jnp.float32), axis=1).astype(jnp.int32)
    dest_row = chosen * capacity + slot_pos
    slot_ids = jnp.arange(experts * capacity, dtype=jnp.int32)
    pair_rows = dest_row.reshape(tok_count, 2)
    place_map = (
        (slot_ids[:, None] == pair_rows[None, :, 0]) | (slot_ids[:, None] == pair_rows[None, :, 1])
    ).astype(jnp.bfloat16)
    outgoing = jnp.dot(place_map, ffn_in, preferred_element_type=jnp.float32).astype(jnp.bfloat16)
    outgoing = outgoing.reshape(experts, capacity, model_width)
    received = lax.all_to_all(outgoing, "expert", split_axis=0, concat_axis=0, tiled=True)
    recv_shape = received.shape
    rows_in = received.reshape(-1, model_width)
    gate_part = jnp.dot(rows_in, w_gate[0], preferred_element_type=jnp.float32)
    up_part = jnp.dot(rows_in, w_up[0], preferred_element_type=jnp.float32)
    inner_act = (jax.nn.silu(gate_part) * up_part).astype(jnp.bfloat16)
    result = jnp.dot(inner_act, w_down[0], preferred_element_type=jnp.float32).astype(jnp.bfloat16)
    returned = lax.all_to_all(
        result.reshape(recv_shape), "expert", split_axis=0, concat_axis=0, tiled=True
    )
    flat_back = returned.reshape(experts * capacity, model_width)
    picks = [
        jnp.dot(
            (pair_rows[:, k][:, None] == slot_ids[None, :]).astype(jnp.bfloat16),
            flat_back,
            preferred_element_type=jnp.bfloat16,
        ).astype(jnp.float32)
        for k in range(2)
    ]
    route_scale = route_weights[0]
    routed = route_scale[:, 0:1] * picks[0] + route_scale[:, 1:2] * picks[1]
    block_out = (hidden_state + routed).astype(jnp.bfloat16)
    return block_out[None]


def solution(mesh):
    in_specs = (
        P("expert", "seq", None),
        P(),
        P(),
        P(),
        P(),
        P(),
        P(),
        P(),
        P(),
        P(),
        P("expert", "seq", None),
        P("expert", "seq", None),
        P("expert", None, None),
        P("expert", None, None),
        P("expert", None, None),
    )
    out_specs = P("expert", "seq", None)
    return jax.shard_map(
        per_device, mesh=mesh, in_specs=in_specs, out_specs=out_specs, check_vma=False
    )
```

```python
import math

import jax
import jax.numpy as jnp
from jax import lax
from jax.sharding import PartitionSpec as P
from jax.experimental import pallas as pl
from jax.experimental.pallas import tpu as pltpu


def from_behind(array, axis, by):
    peers = lax.axis_size(axis)
    pairs = [(i, i + by) for i in range(peers) if 0 <= i + by < peers]
    return lax.ppermute(array, axis, pairs)


def prefix(array, axis, combine, identity):
    peers, place = (lax.axis_size(axis), lax.axis_index(axis))
    everything = jax.tree.map(lambda part: lax.all_gather(part, axis), array)
    start = jax.tree.map(
        lambda part, zero: jnp.broadcast_to(jnp.asarray(zero, part.dtype), part.shape),
        array,
        identity,
    )

    def turn(k, before):
        reached = k < place
        new = combine(before, jax.tree.map(lambda part: part[k], everything))
        return jax.tree.map(lambda a, b: jnp.where(reached, a, b), new, before)

    return lax.fori_loop(0, peers, turn, start)


def rms_scale(values, gain):
    return values * lax.rsqrt(jnp.mean(values * values, axis=-1, keepdims=True) + 1e-05) * gain


def scan_kernel(with_output):
    def body(maps_ref, step_ref, drive_ref, decay_ref, init_ref, *outs):
        states = decay_ref.shape[0]
        tok_count = step_ref.shape[0]
        decay_rows = [decay_ref[n] for n in range(states)]
        if with_output:
            y_ref, end_ref = outs
        else:
            (end_ref,) = outs

        def turn(t, carry):
            step_now = step_ref[t]
            drive_now = step_now * drive_ref[t].astype(jnp.float32)
            base = t * (2 * states)
            total = None
            fresh = []
            for n in range(states):
                value = jnp.exp2(step_now * decay_rows[n]) * carry[n] + drive_now * maps_ref[base + n]
                fresh.append(value)
                if with_output:
                    part = maps_ref[base + states + n] * value
                    total = part if total is None else total + part
            if with_output:
                y_ref[t] = total
            return tuple(fresh)

        if with_output:
            start = tuple(init_ref[n] for n in range(states))
        else:
            start = tuple(jnp.zeros(decay_rows[0].shape, jnp.float32) for n in range(states))
        final = lax.fori_loop(0, tok_count, turn, start, unroll=8)
        for n in range(states):
            end_ref[n] = final[n]

    return body


def local_scan(start_state, step3, drive3, input_map, output_map, decay3, with_output, first, count):
    tok_count, rows, lanes = step3.shape
    states = decay3.shape[0]
    blk = 8
    grid_len = count // blk
    lead = first // blk
    smem = pl.BlockSpec(memory_space=pltpu.SMEM)
    seq_spec = pl.BlockSpec((tok_count, blk, lanes), lambda j: (0, j + lead, 0))
    st_spec = pl.BlockSpec((states, blk, lanes), lambda j: (0, j + lead, 0))
    own_seq = pl.BlockSpec((tok_count, blk, lanes), lambda j: (0, j, 0))
    own_st = pl.BlockSpec((states, blk, lanes), lambda j: (0, j, 0))
    out_shape = [jax.ShapeDtypeStruct((states, count, lanes), jnp.float32)]
    out_specs = [own_st]
    if with_output:
        out_shape.insert(0, jax.ShapeDtypeStruct((tok_count, count, lanes), jnp.float32))
        out_specs.insert(0, own_seq)
    operands = [jnp.concatenate([input_map, output_map], axis=1).reshape(-1), step3, drive3, decay3]
    in_specs = [smem, seq_spec, seq_spec, st_spec]
    body = scan_kernel(with_output)
    if with_output:
        operands.append(start_state)
        in_specs.append(own_st)
    else:
        plain = body
        body = lambda a, b, c, d, *outs: plain(a, b, c, d, None, *outs)
    results = pl.pallas_call(
        body,
        grid=(grid_len,),
        in_specs=in_specs,
        out_specs=out_specs,
        out_shape=out_shape,
    )(*operands)
    if with_output:
        return (results[0], results[-1])
    return (None, results[-1])


def per_device(
    tokens,
    norm_gain,
    conv_weight,
    conv_bias,
    proj_weight,
    dt_weight,
    dt_bias,
    decay_rate,
    skip_gain,
    ffn_gain,
    expert_ids,
    route_weights,
    w_gate,
    w_up,
    w_down,
):
    stream = tokens[0].astype(jnp.float32)
    tok_count = stream.shape[0]
    model_width = stream.shape[1]
    kernel = conv_weight.shape[0]
    low_width = dt_weight.shape[0]
    states = decay_rate.shape[0]
    normed = rms_scale(stream, norm_gain).astype(jnp.bfloat16)
    prior_rows = from_behind(normed[tok_count - (kernel - 1) :], "seq", 1)
    padded = jnp.concatenate([prior_rows, normed], axis=0).astype(jnp.float32)
    conv_sum = jnp.zeros((tok_count, model_width), jnp.float32)
    for offset in range(kernel):
        conv_sum = conv_sum + conv_weight[offset] * padded[offset : offset + tok_count]
    conv_out = jax.nn.silu(conv_sum + conv_bias).astype(jnp.bfloat16)
    projected = jnp.dot(conv_out, proj_weight, preferred_element_type=jnp.float32)
    low_rank = projected[:, :low_width].astype(jnp.bfloat16)
    step_size = jax.nn.softplus(
        jnp.dot(low_rank, dt_weight, preferred_element_type=jnp.float32) + dt_bias
    )
    input_map = projected[:, low_width : low_width + states]
    output_map = projected[:, low_width + states :]
    decay_neg = -decay_rate
    conv_float = conv_out.astype(jnp.float32)
    lanes = 128
    rows = model_width // lanes
    chunks = 2
    count = rows // chunks
    step3 = step_size.reshape(tok_count, rows, lanes)
    drive3 = conv_out.reshape(tok_count, rows, lanes)
    decay3 = (decay_neg * math.log2(math.e)).reshape(states, rows, lanes)
    span3 = jnp.exp(decay_neg * jnp.sum(step_size, axis=0)[None, :]).reshape(states, rows, lanes)
    zero_state = jnp.zeros((states, count, lanes), jnp.float32)
    peers = lax.axis_size("seq")
    inflow = []
    for c in range(chunks):
        _, end_state = local_scan(
            None, step3, drive3, input_map, output_map, decay3, False, c * count, count
        )
        summary = jnp.stack([span3[:, c * count : (c + 1) * count], end_state])
        inflow.append([from_behind(summary, "seq", k) for k in range(peers - 1, 0, -1)])
    pieces = []
    for c in range(chunks):
        incoming = jnp.zeros_like(zero_state)
        for piece in inflow[c]:
            incoming = piece[0] * incoming + piece[1]
        part, _ = local_scan(
            incoming, step3, drive3, input_map, output_map, decay3, True, c * count, count
        )
        pieces.append(part)
    scanned = jnp.concatenate(pieces, axis=1).reshape(tok_count, model_width)
    hidden_state = stream + (scanned + skip_gain * conv_float)
    ffn_in = rms_scale(hidden_state, ffn_gain).astype(jnp.bfloat16)
    owners = lax.axis_size("expert")
    experts = owners * w_gate.shape[0]
    capacity = 4 * tok_count // owners
    chosen = expert_ids[0].reshape(-1)
    onehot = (chosen[:, None] == jnp.arange(experts, dtype=jnp.int32)[None, :]).astype(jnp.bfloat16)
    pair_ids = jnp.arange(chosen.shape[0], dtype=jnp.int32)
    earlier = (pair_ids[:, None] > pair_ids[None, :]).astype(jnp.bfloat16)
    before = jnp.dot(earlier, onehot, preferred_element_type=jnp.float32)
    slot_pos = jnp.sum(before * onehot.astype(jnp.float32), axis=1).astype(jnp.int32)
    dest_row = chosen * capacity + slot_pos
    slot_ids = jnp.arange(experts * capacity, dtype=jnp.int32)
    pair_rows = dest_row.reshape(tok_count, 2)
    place_map = (
        (slot_ids[:, None] == pair_rows[None, :, 0]) | (slot_ids[:, None] == pair_rows[None, :, 1])
    ).astype(jnp.bfloat16)
    outgoing = jnp.dot(place_map, ffn_in, preferred_element_type=jnp.float32).astype(jnp.bfloat16)
    outgoing = outgoing.reshape(experts, capacity, model_width)
    received = lax.all_to_all(outgoing, "expert", split_axis=0, concat_axis=0, tiled=True)
    recv_shape = received.shape
    rows_in = received.reshape(-1, model_width)
    gate_part = jnp.dot(rows_in, w_gate[0], preferred_element_type=jnp.float32)
    up_part = jnp.dot(rows_in, w_up[0], preferred_element_type=jnp.float32)
    inner_act = (jax.nn.silu(gate_part) * up_part).astype(jnp.bfloat16)
    result = jnp.dot(inner_act, w_down[0], preferred_element_type=jnp.float32).astype(jnp.bfloat16)
    returned = lax.all_to_all(
        result.reshape(recv_shape), "expert", split_axis=0, concat_axis=0, tiled=True
    )
    flat_back = returned.reshape(experts * capacity, model_width)
    picks = [
        jnp.dot(
            (pair_rows[:, k][:, None] == slot_ids[None, :]).astype(jnp.bfloat16),
            flat_back,
            preferred_element_type=jnp.bfloat16,
        ).astype(jnp.float32)
        for k in range(2)
    ]
    route_scale = route_weights[0]
    routed = route_scale[:, 0:1] * picks[0] + route_scale[:, 1:2] * picks[1]
    block_out = (hidden_state + routed).astype(jnp.bfloat16)
    return block_out[None]


def solution(mesh):
    in_specs = (
        P("expert", "seq", None),
        P(),
        P(),
        P(),
        P(),
        P(),
        P(),
        P(),
        P(),
        P(),
        P("expert", "seq", None),
        P("expert", "seq", None),
        P("expert", None, None),
        P("expert", None, None),
        P("expert", None, None),
    )
    out_specs = P("expert", "seq", None)
    return jax.shard_map(
        per_device, mesh=mesh, in_specs=in_specs, out_specs=out_specs, check_vma=False
    )
```

```python
import math

import jax
import jax.numpy as jnp
from jax import lax
from jax.sharding import PartitionSpec as P
from jax.experimental import pallas as pl
from jax.experimental.pallas import tpu as pltpu


def from_behind(array, axis, by):
    peers = lax.axis_size(axis)
    pairs = [(i, i + by) for i in range(peers) if 0 <= i + by < peers]
    return lax.ppermute(array, axis, pairs)


def prefix(array, axis, combine, identity):
    peers, place = (lax.axis_size(axis), lax.axis_index(axis))
    everything = jax.tree.map(lambda part: lax.all_gather(part, axis), array)
    start = jax.tree.map(
        lambda part, zero: jnp.broadcast_to(jnp.asarray(zero, part.dtype), part.shape),
        array,
        identity,
    )

    def turn(k, before):
        reached = k < place
        new = combine(before, jax.tree.map(lambda part: part[k], everything))
        return jax.tree.map(lambda a, b: jnp.where(reached, a, b), new, before)

    return lax.fori_loop(0, peers, turn, start)


def rms_scale(values, gain):
    return values * lax.rsqrt(jnp.mean(values * values, axis=-1, keepdims=True) + 1e-05) * gain


def scan_kernel(with_output):
    def body(in_ref, out_ref, step_ref, drive_ref, decay_ref, init_ref, *outs):
        states = decay_ref.shape[0]
        tok_count = step_ref.shape[0]
        decay_rows = [decay_ref[n] for n in range(states)]
        if with_output:
            y_ref, end_ref = outs
        else:
            (end_ref,) = outs

        def turn(t, carry):
            step_now = step_ref[t]
            drive_now = step_now * drive_ref[t].astype(jnp.float32)
            base = t * states
            total = None
            fresh = []
            for n in range(states):
                value = jnp.exp2(step_now * decay_rows[n]) * carry[n] + drive_now * in_ref[base + n]
                fresh.append(value)
                if with_output:
                    part = out_ref[base + n] * value
                    total = part if total is None else total + part
            if with_output:
                y_ref[t] = total
            return tuple(fresh)

        if with_output:
            start = tuple(init_ref[n] for n in range(states))
        else:
            start = tuple(jnp.zeros(decay_rows[0].shape, jnp.float32) for n in range(states))
        final = lax.fori_loop(0, tok_count, turn, start, unroll=8)
        for n in range(states):
            end_ref[n] = final[n]

    return body


def local_scan(
    start_state, step3, drive3, input_map, output_map, decay3, with_output, first, count, into=None
):
    tok_count, rows, lanes = step3.shape
    states = decay3.shape[0]
    blk = 8
    grid_len = count // blk
    lead = first // blk
    smem = pl.BlockSpec(memory_space=pltpu.SMEM)
    seq_spec = pl.BlockSpec((tok_count, blk, lanes), lambda j: (0, j + lead, 0))
    st_spec = pl.BlockSpec((states, blk, lanes), lambda j: (0, j + lead, 0))
    own_seq = pl.BlockSpec((tok_count, blk, lanes), lambda j: (0, j, 0))
    own_st = pl.BlockSpec((states, blk, lanes), lambda j: (0, j, 0))
    out_shape = [jax.ShapeDtypeStruct((states, count, lanes), jnp.float32)]
    out_specs = [own_st]
    if with_output:
        out_shape.insert(0, jax.ShapeDtypeStruct((tok_count, rows, lanes), jnp.float32))
        out_specs.insert(0, seq_spec)
    operands = [input_map.reshape(-1), output_map.reshape(-1), step3, drive3, decay3]
    in_specs = [smem, smem, seq_spec, seq_spec, st_spec]
    body = scan_kernel(with_output)
    aliases = {}
    if with_output:
        operands.append(start_state)
        in_specs.append(own_st)
        if into is not None:
            aliases = {len(operands): 0}
            operands.append(into)
            in_specs.append(pl.BlockSpec(memory_space=pl.ANY))
            plain_out = body
            body = lambda a, b, c, d, e, f, g, *outs: plain_out(a, b, c, d, e, f, *outs)
    else:
        plain = body
        body = lambda a, b, c, d, e, *outs: plain(a, b, c, d, e, None, *outs)
    results = pl.pallas_call(
        body,
        grid=(grid_len,),
        in_specs=in_specs,
        out_specs=out_specs,
        out_shape=out_shape,
        input_output_aliases=aliases,
    )(*operands)
    if with_output:
        return (results[0], results[-1])
    return (None, results[-1])


def per_device(
    tokens,
    norm_gain,
    conv_weight,
    conv_bias,
    proj_weight,
    dt_weight,
    dt_bias,
    decay_rate,
    skip_gain,
    ffn_gain,
    expert_ids,
    route_weights,
    w_gate,
    w_up,
    w_down,
):
    stream = tokens[0].astype(jnp.float32)
    tok_count = stream.shape[0]
    model_width = stream.shape[1]
    kernel = conv_weight.shape[0]
    low_width = dt_weight.shape[0]
    states = decay_rate.shape[0]
    normed = rms_scale(stream, norm_gain).astype(jnp.bfloat16)
    prior_rows = from_behind(normed[tok_count - (kernel - 1) :], "seq", 1)
    padded = jnp.concatenate([prior_rows, normed], axis=0).astype(jnp.float32)
    conv_sum = jnp.zeros((tok_count, model_width), jnp.float32)
    for offset in range(kernel):
        conv_sum = conv_sum + conv_weight[offset] * padded[offset : offset + tok_count]
    conv_out = jax.nn.silu(conv_sum + conv_bias).astype(jnp.bfloat16)
    projected = jnp.dot(conv_out, proj_weight, preferred_element_type=jnp.float32)
    low_rank = projected[:, :low_width].astype(jnp.bfloat16)
    step_size = jax.nn.softplus(
        jnp.dot(low_rank, dt_weight, preferred_element_type=jnp.float32) + dt_bias
    )
    input_map = projected[:, low_width : low_width + states]
    output_map = projected[:, low_width + states :]
    decay_neg = -decay_rate
    conv_float = conv_out.astype(jnp.float32)
    lanes = 128
    rows = model_width // lanes
    chunks = 2
    count = rows // chunks
    step3 = step_size.reshape(tok_count, rows, lanes)
    drive3 = conv_out.reshape(tok_count, rows, lanes)
    decay3 = (decay_neg * math.log2(math.e)).reshape(states, rows, lanes)
    span3 = jnp.exp(decay_neg * jnp.sum(step_size, axis=0)[None, :]).reshape(states, rows, lanes)
    zero_state = jnp.zeros((states, count, lanes), jnp.float32)
    peers = lax.axis_size("seq")
    inflow = []
    for c in range(chunks):
        _, end_state = local_scan(
            None, step3, drive3, input_map, output_map, decay3, False, c * count, count
        )
        summary = jnp.stack([span3[:, c * count : (c + 1) * count], end_state])
        inflow.append([from_behind(summary, "seq", k) for k in range(peers - 1, 0, -1)])
    scanned3 = None
    for c in range(chunks):
        incoming = jnp.zeros_like(zero_state)
        for piece in inflow[c]:
            incoming = piece[0] * incoming + piece[1]
        scanned3, _ = local_scan(
            incoming, step3, drive3, input_map, output_map, decay3, True, c * count, count, scanned3
        )
    scanned = scanned3.reshape(tok_count, model_width)
    hidden_state = stream + (scanned + skip_gain * conv_float)
    ffn_in = rms_scale(hidden_state, ffn_gain).astype(jnp.bfloat16)
    owners = lax.axis_size("expert")
    experts = owners * w_gate.shape[0]
    capacity = 4 * tok_count // owners
    chosen = expert_ids[0].reshape(-1)
    onehot = (chosen[:, None] == jnp.arange(experts, dtype=jnp.int32)[None, :]).astype(jnp.bfloat16)
    pair_ids = jnp.arange(chosen.shape[0], dtype=jnp.int32)
    earlier = (pair_ids[:, None] > pair_ids[None, :]).astype(jnp.bfloat16)
    before = jnp.dot(earlier, onehot, preferred_element_type=jnp.float32)
    slot_pos = jnp.sum(before * onehot.astype(jnp.float32), axis=1).astype(jnp.int32)
    dest_row = chosen * capacity + slot_pos
    slot_ids = jnp.arange(experts * capacity, dtype=jnp.int32)
    pair_rows = dest_row.reshape(tok_count, 2)
    place_map = (
        (slot_ids[:, None] == pair_rows[None, :, 0]) | (slot_ids[:, None] == pair_rows[None, :, 1])
    ).astype(jnp.bfloat16)
    outgoing = jnp.dot(place_map, ffn_in, preferred_element_type=jnp.float32).astype(jnp.bfloat16)
    outgoing = outgoing.reshape(experts, capacity, model_width)
    received = lax.all_to_all(outgoing, "expert", split_axis=0, concat_axis=0, tiled=True)
    recv_shape = received.shape
    rows_in = received.reshape(-1, model_width)
    gate_part = jnp.dot(rows_in, w_gate[0], preferred_element_type=jnp.float32)
    up_part = jnp.dot(rows_in, w_up[0], preferred_element_type=jnp.float32)
    inner_act = (jax.nn.silu(gate_part) * up_part).astype(jnp.bfloat16)
    result = jnp.dot(inner_act, w_down[0], preferred_element_type=jnp.float32).astype(jnp.bfloat16)
    returned = lax.all_to_all(
        result.reshape(recv_shape), "expert", split_axis=0, concat_axis=0, tiled=True
    )
    flat_back = returned.reshape(experts * capacity, model_width)
    picks = [
        jnp.dot(
            (pair_rows[:, k][:, None] == slot_ids[None, :]).astype(jnp.bfloat16),
            flat_back,
            preferred_element_type=jnp.bfloat16,
        ).astype(jnp.float32)
        for k in range(2)
    ]
    route_scale = route_weights[0]
    routed = route_scale[:, 0:1] * picks[0] + route_scale[:, 1:2] * picks[1]
    block_out = (hidden_state + routed).astype(jnp.bfloat16)
    return block_out[None]


def solution(mesh):
    in_specs = (
        P("expert", "seq", None),
        P(),
        P(),
        P(),
        P(),
        P(),
        P(),
        P(),
        P(),
        P(),
        P("expert", "seq", None),
        P("expert", "seq", None),
        P("expert", None, None),
        P("expert", None, None),
        P("expert", None, None),
    )
    out_specs = P("expert", "seq", None)
    return jax.shard_map(
        per_device, mesh=mesh, in_specs=in_specs, out_specs=out_specs, check_vma=False
    )
```

```python
import math

import jax
import jax.numpy as jnp
from jax import lax
from jax.sharding import PartitionSpec as P
from jax.experimental import pallas as pl
from jax.experimental.pallas import tpu as pltpu


def from_behind(array, axis, by):
    peers = lax.axis_size(axis)
    pairs = [(i, i + by) for i in range(peers) if 0 <= i + by < peers]
    return lax.ppermute(array, axis, pairs)


def prefix(array, axis, combine, identity):
    peers, place = (lax.axis_size(axis), lax.axis_index(axis))
    everything = jax.tree.map(lambda part: lax.all_gather(part, axis), array)
    start = jax.tree.map(
        lambda part, zero: jnp.broadcast_to(jnp.asarray(zero, part.dtype), part.shape),
        array,
        identity,
    )

    def turn(k, before):
        reached = k < place
        new = combine(before, jax.tree.map(lambda part: part[k], everything))
        return jax.tree.map(lambda a, b: jnp.where(reached, a, b), new, before)

    return lax.fori_loop(0, peers, turn, start)


def rms_scale(values, gain):
    return values * lax.rsqrt(jnp.mean(values * values, axis=-1, keepdims=True) + 1e-05) * gain


def scan_kernel(with_output):
    def body(in_ref, out_ref, step_ref, drive_ref, decay_ref, init_ref, *outs):
        states = decay_ref.shape[0]
        tok_count = step_ref.shape[0]
        decay_rows = [decay_ref[n] for n in range(states)]
        if with_output:
            y_ref, end_ref = outs
        else:
            (end_ref,) = outs

        def turn(t, carry):
            step_now = step_ref[t]
            drive_now = step_now * drive_ref[t].astype(jnp.float32)
            base = t * states
            total = None
            fresh = []
            for n in range(states):
                value = jnp.exp2(step_now * decay_rows[n]) * carry[n] + drive_now * in_ref[base + n]
                fresh.append(value)
                if with_output:
                    part = out_ref[base + n] * value
                    total = part if total is None else total + part
            if with_output:
                y_ref[t] = total
                return tuple(fresh)
            return tuple(fresh) + (carry[states] + step_now,)

        if with_output:
            start = tuple(init_ref[n] for n in range(states))
        else:
            start = tuple(jnp.zeros(decay_rows[0].shape, jnp.float32) for n in range(states + 1))
        final = lax.fori_loop(0, tok_count, turn, start, unroll=8)
        if with_output:
            for n in range(states):
                end_ref[n] = final[n]
        else:
            for n in range(states):
                end_ref[0, n] = jnp.exp2(decay_rows[n] * final[states])
                end_ref[1, n] = final[n]

    return body


def local_scan(
    start_state, step3, drive3, input_map, output_map, decay3, with_output, first, count, into=None
):
    tok_count, rows, lanes = step3.shape
    states = decay3.shape[0]
    blk = 8
    grid_len = count // blk
    lead = first // blk
    smem = pl.BlockSpec(memory_space=pltpu.SMEM)
    seq_spec = pl.BlockSpec((tok_count, blk, lanes), lambda j: (0, j + lead, 0))
    st_spec = pl.BlockSpec((states, blk, lanes), lambda j: (0, j + lead, 0))
    own_seq = pl.BlockSpec((tok_count, blk, lanes), lambda j: (0, j, 0))
    own_st = pl.BlockSpec((states, blk, lanes), lambda j: (0, j, 0))
    if with_output:
        out_shape = [jax.ShapeDtypeStruct((states, count, lanes), jnp.float32)]
        out_specs = [own_st]
    else:
        out_shape = [jax.ShapeDtypeStruct((2, states, count, lanes), jnp.float32)]
        out_specs = [pl.BlockSpec((2, states, blk, lanes), lambda j: (0, 0, j, 0))]
    if with_output:
        out_shape.insert(0, jax.ShapeDtypeStruct((tok_count, rows, lanes), jnp.float32))
        out_specs.insert(0, seq_spec)
    operands = [input_map.reshape(-1), output_map.reshape(-1), step3, drive3, decay3]
    in_specs = [smem, smem, seq_spec, seq_spec, st_spec]
    body = scan_kernel(with_output)
    aliases = {}
    if with_output:
        operands.append(start_state)
        in_specs.append(own_st)
        if into is not None:
            aliases = {len(operands): 0}
            operands.append(into)
            in_specs.append(pl.BlockSpec(memory_space=pl.ANY))
            plain_out = body
            body = lambda a, b, c, d, e, f, g, *outs: plain_out(a, b, c, d, e, f, *outs)
    else:
        plain = body
        body = lambda a, b, c, d, e, *outs: plain(a, b, c, d, e, None, *outs)
    results = pl.pallas_call(
        body,
        grid=(grid_len,),
        in_specs=in_specs,
        out_specs=out_specs,
        out_shape=out_shape,
        input_output_aliases=aliases,
    )(*operands)
    if with_output:
        return (results[0], results[-1])
    return (None, results[-1])


def per_device(
    tokens,
    norm_gain,
    conv_weight,
    conv_bias,
    proj_weight,
    dt_weight,
    dt_bias,
    decay_rate,
    skip_gain,
    ffn_gain,
    expert_ids,
    route_weights,
    w_gate,
    w_up,
    w_down,
):
    stream = tokens[0].astype(jnp.float32)
    tok_count = stream.shape[0]
    model_width = stream.shape[1]
    kernel = conv_weight.shape[0]
    low_width = dt_weight.shape[0]
    states = decay_rate.shape[0]
    normed = rms_scale(stream, norm_gain).astype(jnp.bfloat16)
    prior_rows = from_behind(normed[tok_count - (kernel - 1) :], "seq", 1)
    padded = jnp.concatenate([prior_rows, normed], axis=0).astype(jnp.float32)
    conv_sum = jnp.zeros((tok_count, model_width), jnp.float32)
    for offset in range(kernel):
        conv_sum = conv_sum + conv_weight[offset] * padded[offset : offset + tok_count]
    conv_out = jax.nn.silu(conv_sum + conv_bias).astype(jnp.bfloat16)
    projected = jnp.dot(conv_out, proj_weight, preferred_element_type=jnp.float32)
    low_rank = projected[:, :low_width].astype(jnp.bfloat16)
    step_size = jax.nn.softplus(
        jnp.dot(low_rank, dt_weight, preferred_element_type=jnp.float32) + dt_bias
    )
    input_map = projected[:, low_width : low_width + states]
    output_map = projected[:, low_width + states :]
    decay_neg = -decay_rate
    conv_float = conv_out.astype(jnp.float32)
    lanes = 128
    rows = model_width // lanes
    chunks = 2
    count = rows // chunks
    step3 = step_size.reshape(tok_count, rows, lanes)
    drive3 = conv_out.reshape(tok_count, rows, lanes)
    decay3 = (decay_neg * math.log2(math.e)).reshape(states, rows, lanes)
    zero_state = jnp.zeros((states, count, lanes), jnp.float32)
    peers = lax.axis_size("seq")
    inflow = []
    for c in range(chunks):
        _, end_state = local_scan(
            None, step3, drive3, input_map, output_map, decay3, False, c * count, count
        )
        summary = end_state
        inflow.append([from_behind(summary, "seq", k) for k in range(peers - 1, 0, -1)])
    scanned3 = None
    for c in range(chunks):
        incoming = jnp.zeros_like(zero_state)
        for piece in inflow[c]:
            incoming = piece[0] * incoming + piece[1]
        scanned3, _ = local_scan(
            incoming, step3, drive3, input_map, output_map, decay3, True, c * count, count, scanned3
        )
    scanned = scanned3.reshape(tok_count, model_width)
    hidden_state = stream + (scanned + skip_gain * conv_float)
    ffn_in = rms_scale(hidden_state, ffn_gain).astype(jnp.bfloat16)
    owners = lax.axis_size("expert")
    experts = owners * w_gate.shape[0]
    capacity = 4 * tok_count // owners
    chosen = expert_ids[0].reshape(-1)
    onehot = (chosen[:, None] == jnp.arange(experts, dtype=jnp.int32)[None, :]).astype(jnp.bfloat16)
    pair_ids = jnp.arange(chosen.shape[0], dtype=jnp.int32)
    earlier = (pair_ids[:, None] > pair_ids[None, :]).astype(jnp.bfloat16)
    before = jnp.dot(earlier, onehot, preferred_element_type=jnp.float32)
    slot_pos = jnp.sum(before * onehot.astype(jnp.float32), axis=1).astype(jnp.int32)
    dest_row = chosen * capacity + slot_pos
    slot_ids = jnp.arange(experts * capacity, dtype=jnp.int32)
    pair_rows = dest_row.reshape(tok_count, 2)
    place_map = (
        (slot_ids[:, None] == pair_rows[None, :, 0]) | (slot_ids[:, None] == pair_rows[None, :, 1])
    ).astype(jnp.bfloat16)
    outgoing = jnp.dot(place_map, ffn_in, preferred_element_type=jnp.float32).astype(jnp.bfloat16)
    outgoing = outgoing.reshape(experts, capacity, model_width)
    received = lax.all_to_all(outgoing, "expert", split_axis=0, concat_axis=0, tiled=True)
    recv_shape = received.shape
    rows_in = received.reshape(-1, model_width)
    gate_part = jnp.dot(rows_in, w_gate[0], preferred_element_type=jnp.float32)
    up_part = jnp.dot(rows_in, w_up[0], preferred_element_type=jnp.float32)
    inner_act = (jax.nn.silu(gate_part) * up_part).astype(jnp.bfloat16)
    result = jnp.dot(inner_act, w_down[0], preferred_element_type=jnp.float32).astype(jnp.bfloat16)
    returned = lax.all_to_all(
        result.reshape(recv_shape), "expert", split_axis=0, concat_axis=0, tiled=True
    )
    flat_back = returned.reshape(experts * capacity, model_width)
    picks = [
        jnp.dot(
            (pair_rows[:, k][:, None] == slot_ids[None, :]).astype(jnp.bfloat16),
            flat_back,
            preferred_element_type=jnp.bfloat16,
        ).astype(jnp.float32)
        for k in range(2)
    ]
    route_scale = route_weights[0]
    routed = route_scale[:, 0:1] * picks[0] + route_scale[:, 1:2] * picks[1]
    block_out = (hidden_state + routed).astype(jnp.bfloat16)
    return block_out[None]


def solution(mesh):
    in_specs = (
        P("expert", "seq", None),
        P(),
        P(),
        P(),
        P(),
        P(),
        P(),
        P(),
        P(),
        P(),
        P("expert", "seq", None),
        P("expert", "seq", None),
        P("expert", None, None),
        P("expert", None, None),
        P("expert", None, None),
    )
    out_specs = P("expert", "seq", None)
    return jax.shard_map(
        per_device, mesh=mesh, in_specs=in_specs, out_specs=out_specs, check_vma=False
    )
```

```python
import math

import jax
import jax.numpy as jnp
from jax import lax
from jax.sharding import PartitionSpec as P
from jax.experimental import pallas as pl
from jax.experimental.pallas import tpu as pltpu


def from_behind(array, axis, by):
    peers = lax.axis_size(axis)
    pairs = [(i, i + by) for i in range(peers) if 0 <= i + by < peers]
    return lax.ppermute(array, axis, pairs)


def prefix(array, axis, combine, identity):
    peers, place = (lax.axis_size(axis), lax.axis_index(axis))
    everything = jax.tree.map(lambda part: lax.all_gather(part, axis), array)
    start = jax.tree.map(
        lambda part, zero: jnp.broadcast_to(jnp.asarray(zero, part.dtype), part.shape),
        array,
        identity,
    )

    def turn(k, before):
        reached = k < place
        new = combine(before, jax.tree.map(lambda part: part[k], everything))
        return jax.tree.map(lambda a, b: jnp.where(reached, a, b), new, before)

    return lax.fori_loop(0, peers, turn, start)


def rms_scale(values, gain):
    return values * lax.rsqrt(jnp.mean(values * values, axis=-1, keepdims=True) + 1e-05) * gain


def scan_kernel(with_output):
    def body(in_ref, out_ref, step_ref, drive_ref, decay_ref, init_ref, *outs):
        states = decay_ref.shape[0]
        tok_count = step_ref.shape[0]
        decay_rows = [decay_ref[n] for n in range(states)]
        if with_output:
            y_ref, end_ref = outs
        else:
            (end_ref,) = outs

        def turn(t, carry):
            step_now = step_ref[t]
            drive_now = step_now * drive_ref[t].astype(jnp.float32)
            base = t * states
            total = None
            fresh = []
            for n in range(states):
                value = jnp.exp2(step_now * decay_rows[n]) * carry[n] + drive_now * in_ref[base + n]
                fresh.append(value)
                if with_output:
                    part = out_ref[base + n] * value
                    total = part if total is None else total + part
            if with_output:
                y_ref[t] = total
                return tuple(fresh)
            return tuple(fresh) + (carry[states] + step_now,)

        if with_output:
            start = []
            for n in range(states):
                value = jnp.zeros(decay_rows[0].shape, jnp.float32)
                for piece in init_ref:
                    value = piece[0, n] * value + piece[1, n]
                start.append(value)
            start = tuple(start)
        else:
            start = tuple(jnp.zeros(decay_rows[0].shape, jnp.float32) for n in range(states + 1))
        final = lax.fori_loop(0, tok_count, turn, start, unroll=8)
        if with_output:
            for n in range(states):
                end_ref[n] = final[n]
        else:
            for n in range(states):
                end_ref[0, n] = jnp.exp2(decay_rows[n] * final[states])
                end_ref[1, n] = final[n]

    return body


def local_scan(
    start_state, step3, drive3, input_map, output_map, decay3, with_output, first, count, into=None
):
    tok_count, rows, lanes = step3.shape
    states = decay3.shape[0]
    blk = 8
    grid_len = count // blk
    lead = first // blk
    smem = pl.BlockSpec(memory_space=pltpu.SMEM)
    seq_spec = pl.BlockSpec((tok_count, blk, lanes), lambda j: (0, j + lead, 0))
    st_spec = pl.BlockSpec((states, blk, lanes), lambda j: (0, j + lead, 0))
    own_seq = pl.BlockSpec((tok_count, blk, lanes), lambda j: (0, j, 0))
    own_st = pl.BlockSpec((states, blk, lanes), lambda j: (0, j, 0))
    if with_output:
        out_shape = [jax.ShapeDtypeStruct((states, count, lanes), jnp.float32)]
        out_specs = [own_st]
    else:
        out_shape = [jax.ShapeDtypeStruct((2, states, count, lanes), jnp.float32)]
        out_specs = [pl.BlockSpec((2, states, blk, lanes), lambda j: (0, 0, j, 0))]
    if with_output:
        out_shape.insert(0, jax.ShapeDtypeStruct((tok_count, rows, lanes), jnp.float32))
        out_specs.insert(0, seq_spec)
    operands = [input_map.reshape(-1), output_map.reshape(-1), step3, drive3, decay3]
    in_specs = [smem, smem, seq_spec, seq_spec, st_spec]
    aliases = {}
    plain = scan_kernel(with_output)
    extra = 0
    if with_output:
        piece_spec = pl.BlockSpec((2, states, blk, lanes), lambda j: (0, 0, j, 0))
        operands.extend(start_state)
        in_specs.extend([piece_spec] * len(start_state))
        if into is not None:
            aliases = {len(operands): 0}
            operands.append(into)
            in_specs.append(pl.BlockSpec(memory_space=pl.ANY))
            extra = 1
    held = len(start_state) if with_output else 0

    def body(*refs):
        lead_refs = refs[:5]
        pieces = tuple(refs[5 : 5 + held]) if with_output else None
        return plain(*lead_refs, pieces, *refs[5 + held + extra :])

    results = pl.pallas_call(
        body,
        grid=(grid_len,),
        in_specs=in_specs,
        out_specs=out_specs,
        out_shape=out_shape,
        input_output_aliases=aliases,
    )(*operands)
    if with_output:
        return (results[0], results[-1])
    return (None, results[-1])


def per_device(
    tokens,
    norm_gain,
    conv_weight,
    conv_bias,
    proj_weight,
    dt_weight,
    dt_bias,
    decay_rate,
    skip_gain,
    ffn_gain,
    expert_ids,
    route_weights,
    w_gate,
    w_up,
    w_down,
):
    stream = tokens[0].astype(jnp.float32)
    tok_count = stream.shape[0]
    model_width = stream.shape[1]
    kernel = conv_weight.shape[0]
    low_width = dt_weight.shape[0]
    states = decay_rate.shape[0]
    normed = rms_scale(stream, norm_gain).astype(jnp.bfloat16)
    prior_rows = from_behind(normed[tok_count - (kernel - 1) :], "seq", 1)
    padded = jnp.concatenate([prior_rows, normed], axis=0).astype(jnp.float32)
    conv_sum = jnp.zeros((tok_count, model_width), jnp.float32)
    for offset in range(kernel):
        conv_sum = conv_sum + conv_weight[offset] * padded[offset : offset + tok_count]
    conv_out = jax.nn.silu(conv_sum + conv_bias).astype(jnp.bfloat16)
    projected = jnp.dot(conv_out, proj_weight, preferred_element_type=jnp.float32)
    low_rank = projected[:, :low_width].astype(jnp.bfloat16)
    step_size = jax.nn.softplus(
        jnp.dot(low_rank, dt_weight, preferred_element_type=jnp.float32) + dt_bias
    )
    input_map = projected[:, low_width : low_width + states]
    output_map = projected[:, low_width + states :]
    decay_neg = -decay_rate
    conv_float = conv_out.astype(jnp.float32)
    lanes = 128
    rows = model_width // lanes
    chunks = 2
    count = rows // chunks
    step3 = step_size.reshape(tok_count, rows, lanes)
    drive3 = conv_out.reshape(tok_count, rows, lanes)
    decay3 = (decay_neg * math.log2(math.e)).reshape(states, rows, lanes)
    zero_state = jnp.zeros((states, count, lanes), jnp.float32)
    peers = lax.axis_size("seq")
    inflow = []
    for c in range(chunks):
        _, end_state = local_scan(
            None, step3, drive3, input_map, output_map, decay3, False, c * count, count
        )
        summary = end_state
        inflow.append([from_behind(summary, "seq", k) for k in range(peers - 1, 0, -1)])
    scanned3 = None
    for c in range(chunks):
        incoming = inflow[c]
        scanned3, _ = local_scan(
            incoming, step3, drive3, input_map, output_map, decay3, True, c * count, count, scanned3
        )
    scanned = scanned3.reshape(tok_count, model_width)
    hidden_state = stream + (scanned + skip_gain * conv_float)
    ffn_in = rms_scale(hidden_state, ffn_gain).astype(jnp.bfloat16)
    owners = lax.axis_size("expert")
    experts = owners * w_gate.shape[0]
    capacity = 4 * tok_count // owners
    chosen = expert_ids[0].reshape(-1)
    onehot = (chosen[:, None] == jnp.arange(experts, dtype=jnp.int32)[None, :]).astype(jnp.bfloat16)
    pair_ids = jnp.arange(chosen.shape[0], dtype=jnp.int32)
    earlier = (pair_ids[:, None] > pair_ids[None, :]).astype(jnp.bfloat16)
    before = jnp.dot(earlier, onehot, preferred_element_type=jnp.float32)
    slot_pos = jnp.sum(before * onehot.astype(jnp.float32), axis=1).astype(jnp.int32)
    dest_row = chosen * capacity + slot_pos
    slot_ids = jnp.arange(experts * capacity, dtype=jnp.int32)
    pair_rows = dest_row.reshape(tok_count, 2)
    place_map = (
        (slot_ids[:, None] == pair_rows[None, :, 0]) | (slot_ids[:, None] == pair_rows[None, :, 1])
    ).astype(jnp.bfloat16)
    outgoing = jnp.dot(place_map, ffn_in, preferred_element_type=jnp.float32).astype(jnp.bfloat16)
    outgoing = outgoing.reshape(experts, capacity, model_width)
    received = lax.all_to_all(outgoing, "expert", split_axis=0, concat_axis=0, tiled=True)
    recv_shape = received.shape
    rows_in = received.reshape(-1, model_width)
    gate_part = jnp.dot(rows_in, w_gate[0], preferred_element_type=jnp.float32)
    up_part = jnp.dot(rows_in, w_up[0], preferred_element_type=jnp.float32)
    inner_act = (jax.nn.silu(gate_part) * up_part).astype(jnp.bfloat16)
    result = jnp.dot(inner_act, w_down[0], preferred_element_type=jnp.float32).astype(jnp.bfloat16)
    returned = lax.all_to_all(
        result.reshape(recv_shape), "expert", split_axis=0, concat_axis=0, tiled=True
    )
    flat_back = returned.reshape(experts * capacity, model_width)
    picks = [
        jnp.dot(
            (pair_rows[:, k][:, None] == slot_ids[None, :]).astype(jnp.bfloat16),
            flat_back,
            preferred_element_type=jnp.bfloat16,
        ).astype(jnp.float32)
        for k in range(2)
    ]
    route_scale = route_weights[0]
    routed = route_scale[:, 0:1] * picks[0] + route_scale[:, 1:2] * picks[1]
    block_out = (hidden_state + routed).astype(jnp.bfloat16)
    return block_out[None]


def solution(mesh):
    in_specs = (
        P("expert", "seq", None),
        P(),
        P(),
        P(),
        P(),
        P(),
        P(),
        P(),
        P(),
        P(),
        P("expert", "seq", None),
        P("expert", "seq", None),
        P("expert", None, None),
        P("expert", None, None),
        P("expert", None, None),
    )
    out_specs = P("expert", "seq", None)
    return jax.shard_map(
        per_device, mesh=mesh, in_specs=in_specs, out_specs=out_specs, check_vma=False
    )
```

```python
import math

import jax
import jax.numpy as jnp
from jax import lax
from jax.sharding import PartitionSpec as P
from jax.experimental import pallas as pl
from jax.experimental.pallas import tpu as pltpu


def from_behind(array, axis, by):
    peers = lax.axis_size(axis)
    pairs = [(i, i + by) for i in range(peers) if 0 <= i + by < peers]
    return lax.ppermute(array, axis, pairs)


def prefix(array, axis, combine, identity):
    peers, place = (lax.axis_size(axis), lax.axis_index(axis))
    everything = jax.tree.map(lambda part: lax.all_gather(part, axis), array)
    start = jax.tree.map(
        lambda part, zero: jnp.broadcast_to(jnp.asarray(zero, part.dtype), part.shape),
        array,
        identity,
    )

    def turn(k, before):
        reached = k < place
        new = combine(before, jax.tree.map(lambda part: part[k], everything))
        return jax.tree.map(lambda a, b: jnp.where(reached, a, b), new, before)

    return lax.fori_loop(0, peers, turn, start)


def rms_scale(values, gain):
    return values * lax.rsqrt(jnp.mean(values * values, axis=-1, keepdims=True) + 1e-05) * gain


def scan_kernel(with_output):
    def body(maps_ref, step_ref, drive_ref, decay_ref, init_ref, *outs):
        states = decay_ref.shape[0]
        tok_count = step_ref.shape[0]
        decay_rows = [decay_ref[n] for n in range(states)]
        if with_output:
            y_ref, end_ref = outs
        else:
            (end_ref,) = outs

        def turn(t, carry):
            step_now = step_ref[t]
            drive_now = step_now * drive_ref[t].astype(jnp.float32)
            base = t * (2 * states)
            total = None
            fresh = []
            for n in range(states):
                value = jnp.exp2(step_now * decay_rows[n]) * carry[n] + drive_now * maps_ref[base + n]
                fresh.append(value)
                if with_output:
                    part = maps_ref[base + states + n] * value
                    total = part if total is None else total + part
            if with_output:
                y_ref[t] = total
                return tuple(fresh)
            return tuple(fresh) + (carry[states] + step_now,)

        if with_output:
            start = []
            for n in range(states):
                value = jnp.zeros(decay_rows[0].shape, jnp.float32)
                for piece in init_ref:
                    value = piece[0, n] * value + piece[1, n]
                start.append(value)
            start = tuple(start)
        else:
            start = tuple(jnp.zeros(decay_rows[0].shape, jnp.float32) for n in range(states + 1))
        final = lax.fori_loop(0, tok_count, turn, start, unroll=8)
        if with_output:
            for n in range(states):
                end_ref[n] = final[n]
        else:
            for n in range(states):
                end_ref[0, n] = jnp.exp2(decay_rows[n] * final[states])
                end_ref[1, n] = final[n]

    return body


def local_scan(
    start_state, step3, drive3, input_map, output_map, decay3, with_output, first, count, into=None
):
    tok_count, rows, lanes = step3.shape
    states = decay3.shape[0]
    blk = 8
    grid_len = count // blk
    lead = first // blk
    smem = pl.BlockSpec(memory_space=pltpu.SMEM)
    seq_spec = pl.BlockSpec((tok_count, blk, lanes), lambda j: (0, j + lead, 0))
    st_spec = pl.BlockSpec((states, blk, lanes), lambda j: (0, j + lead, 0))
    own_seq = pl.BlockSpec((tok_count, blk, lanes), lambda j: (0, j, 0))
    own_st = pl.BlockSpec((states, blk, lanes), lambda j: (0, j, 0))
    if with_output:
        out_shape = [jax.ShapeDtypeStruct((states, count, lanes), jnp.float32)]
        out_specs = [own_st]
    else:
        out_shape = [jax.ShapeDtypeStruct((2, states, count, lanes), jnp.float32)]
        out_specs = [pl.BlockSpec((2, states, blk, lanes), lambda j: (0, 0, j, 0))]
    if with_output:
        out_shape.insert(0, jax.ShapeDtypeStruct((tok_count, rows, lanes), jnp.float32))
        out_specs.insert(0, seq_spec)
    operands = [jnp.concatenate([input_map, output_map], axis=1).reshape(-1), step3, drive3, decay3]
    in_specs = [smem, seq_spec, seq_spec, st_spec]
    aliases = {}
    plain = scan_kernel(with_output)
    extra = 0
    if with_output:
        piece_spec = pl.BlockSpec((2, states, blk, lanes), lambda j: (0, 0, j, 0))
        operands.extend(start_state)
        in_specs.extend([piece_spec] * len(start_state))
        if into is not None:
            aliases = {len(operands): 0}
            operands.append(into)
            in_specs.append(pl.BlockSpec(memory_space=pl.ANY))
            extra = 1
    held = len(start_state) if with_output else 0

    def body(*refs):
        lead_refs = refs[:4]
        pieces = tuple(refs[4 : 4 + held]) if with_output else None
        return plain(*lead_refs, pieces, *refs[4 + held + extra :])

    results = pl.pallas_call(
        body,
        grid=(grid_len,),
        in_specs=in_specs,
        out_specs=out_specs,
        out_shape=out_shape,
        input_output_aliases=aliases,
    )(*operands)
    if with_output:
        return (results[0], results[-1])
    return (None, results[-1])


def per_device(
    tokens,
    norm_gain,
    conv_weight,
    conv_bias,
    proj_weight,
    dt_weight,
    dt_bias,
    decay_rate,
    skip_gain,
    ffn_gain,
    expert_ids,
    route_weights,
    w_gate,
    w_up,
    w_down,
):
    stream = tokens[0].astype(jnp.float32)
    tok_count = stream.shape[0]
    model_width = stream.shape[1]
    kernel = conv_weight.shape[0]
    low_width = dt_weight.shape[0]
    states = decay_rate.shape[0]
    normed = rms_scale(stream, norm_gain).astype(jnp.bfloat16)
    prior_rows = from_behind(normed[tok_count - (kernel - 1) :], "seq", 1)
    padded = jnp.concatenate([prior_rows, normed], axis=0).astype(jnp.float32)
    conv_sum = jnp.zeros((tok_count, model_width), jnp.float32)
    for offset in range(kernel):
        conv_sum = conv_sum + conv_weight[offset] * padded[offset : offset + tok_count]
    conv_out = jax.nn.silu(conv_sum + conv_bias).astype(jnp.bfloat16)
    projected = jnp.dot(conv_out, proj_weight, preferred_element_type=jnp.float32)
    low_rank = projected[:, :low_width].astype(jnp.bfloat16)
    step_size = jax.nn.softplus(
        jnp.dot(low_rank, dt_weight, preferred_element_type=jnp.float32) + dt_bias
    )
    input_map = projected[:, low_width : low_width + states]
    output_map = projected[:, low_width + states :]
    decay_neg = -decay_rate
    conv_float = conv_out.astype(jnp.float32)
    lanes = 128
    rows = model_width // lanes
    chunks = 2
    count = rows // chunks
    step3 = step_size.reshape(tok_count, rows, lanes)
    drive3 = conv_out.reshape(tok_count, rows, lanes)
    decay3 = (decay_neg * math.log2(math.e)).reshape(states, rows, lanes)
    zero_state = jnp.zeros((states, count, lanes), jnp.float32)
    peers = lax.axis_size("seq")
    inflow = []
    for c in range(chunks):
        _, end_state = local_scan(
            None, step3, drive3, input_map, output_map, decay3, False, c * count, count
        )
        summary = end_state
        inflow.append([from_behind(summary, "seq", k) for k in range(peers - 1, 0, -1)])
    scanned3 = None
    for c in range(chunks):
        incoming = inflow[c]
        scanned3, _ = local_scan(
            incoming, step3, drive3, input_map, output_map, decay3, True, c * count, count, scanned3
        )
    scanned = scanned3.reshape(tok_count, model_width)
    hidden_state = stream + (scanned + skip_gain * conv_float)
    ffn_in = rms_scale(hidden_state, ffn_gain).astype(jnp.bfloat16)
    owners = lax.axis_size("expert")
    experts = owners * w_gate.shape[0]
    capacity = 4 * tok_count // owners
    chosen = expert_ids[0].reshape(-1)
    onehot = (chosen[:, None] == jnp.arange(experts, dtype=jnp.int32)[None, :]).astype(jnp.bfloat16)
    pair_ids = jnp.arange(chosen.shape[0], dtype=jnp.int32)
    earlier = (pair_ids[:, None] > pair_ids[None, :]).astype(jnp.bfloat16)
    before = jnp.dot(earlier, onehot, preferred_element_type=jnp.float32)
    slot_pos = jnp.sum(before * onehot.astype(jnp.float32), axis=1).astype(jnp.int32)
    dest_row = chosen * capacity + slot_pos
    slot_ids = jnp.arange(experts * capacity, dtype=jnp.int32)
    pair_rows = dest_row.reshape(tok_count, 2)
    place_map = (
        (slot_ids[:, None] == pair_rows[None, :, 0]) | (slot_ids[:, None] == pair_rows[None, :, 1])
    ).astype(jnp.bfloat16)
    outgoing = jnp.dot(place_map, ffn_in, preferred_element_type=jnp.float32).astype(jnp.bfloat16)
    outgoing = outgoing.reshape(experts, capacity, model_width)
    received = lax.all_to_all(outgoing, "expert", split_axis=0, concat_axis=0, tiled=True)
    recv_shape = received.shape
    rows_in = received.reshape(-1, model_width)
    gate_part = jnp.dot(rows_in, w_gate[0], preferred_element_type=jnp.float32)
    up_part = jnp.dot(rows_in, w_up[0], preferred_element_type=jnp.float32)
    inner_act = (jax.nn.silu(gate_part) * up_part).astype(jnp.bfloat16)
    result = jnp.dot(inner_act, w_down[0], preferred_element_type=jnp.float32).astype(jnp.bfloat16)
    returned = lax.all_to_all(
        result.reshape(recv_shape), "expert", split_axis=0, concat_axis=0, tiled=True
    )
    flat_back = returned.reshape(experts * capacity, model_width)
    picks = [
        jnp.dot(
            (pair_rows[:, k][:, None] == slot_ids[None, :]).astype(jnp.bfloat16),
            flat_back,
            preferred_element_type=jnp.bfloat16,
        ).astype(jnp.float32)
        for k in range(2)
    ]
    route_scale = route_weights[0]
    routed = route_scale[:, 0:1] * picks[0] + route_scale[:, 1:2] * picks[1]
    block_out = (hidden_state + routed).astype(jnp.bfloat16)
    return block_out[None]


def solution(mesh):
    in_specs = (
        P("expert", "seq", None),
        P(),
        P(),
        P(),
        P(),
        P(),
        P(),
        P(),
        P(),
        P(),
        P("expert", "seq", None),
        P("expert", "seq", None),
        P("expert", None, None),
        P("expert", None, None),
        P("expert", None, None),
    )
    out_specs = P("expert", "seq", None)
    return jax.shard_map(
        per_device, mesh=mesh, in_specs=in_specs, out_specs=out_specs, check_vma=False
    )
```

```python
import math

import jax
import jax.numpy as jnp
from jax import lax
from jax.sharding import PartitionSpec as P
from jax.experimental import pallas as pl
from jax.experimental.pallas import tpu as pltpu


def from_behind(array, axis, by):
    peers = lax.axis_size(axis)
    pairs = [(i, i + by) for i in range(peers) if 0 <= i + by < peers]
    return lax.ppermute(array, axis, pairs)


def prefix(array, axis, combine, identity):
    peers, place = (lax.axis_size(axis), lax.axis_index(axis))
    everything = jax.tree.map(lambda part: lax.all_gather(part, axis), array)
    start = jax.tree.map(
        lambda part, zero: jnp.broadcast_to(jnp.asarray(zero, part.dtype), part.shape),
        array,
        identity,
    )

    def turn(k, before):
        reached = k < place
        new = combine(before, jax.tree.map(lambda part: part[k], everything))
        return jax.tree.map(lambda a, b: jnp.where(reached, a, b), new, before)

    return lax.fori_loop(0, peers, turn, start)


def rms_scale(values, gain):
    return values * lax.rsqrt(jnp.mean(values * values, axis=-1, keepdims=True) + 1e-05) * gain


def scan_kernel(with_output):
    def body(maps_ref, step_ref, drive_ref, decay_ref, init_ref, *outs):
        states = decay_ref.shape[0]
        tok_count = step_ref.shape[0]
        decay_rows = [decay_ref[n] for n in range(states)]
        if with_output:
            y_ref, end_ref = outs
        else:
            (end_ref,) = outs

        def turn(t, carry):
            step_now = step_ref[t]
            drive_now = step_now * drive_ref[t].astype(jnp.float32)
            base = t * (2 * states)
            total = None
            fresh = []
            for n in range(states):
                value = jnp.exp2(step_now * decay_rows[n]) * carry[n] + drive_now * maps_ref[base + n]
                fresh.append(value)
                if with_output:
                    part = maps_ref[base + states + n] * value
                    total = part if total is None else total + part
            if with_output:
                y_ref[t] = total
                return tuple(fresh)
            return tuple(fresh) + (carry[states] + step_now,)

        if with_output:
            start = []
            for n in range(states):
                value = jnp.zeros(decay_rows[0].shape, jnp.float32)
                for piece in init_ref:
                    value = piece[0, n] * value + piece[1, n]
                start.append(value)
            start = tuple(start)
        else:
            start = tuple(jnp.zeros(decay_rows[0].shape, jnp.float32) for n in range(states + 1))
        final = lax.fori_loop(0, tok_count, turn, start, unroll=16)
        if with_output:
            for n in range(states):
                end_ref[n] = final[n]
        else:
            for n in range(states):
                end_ref[0, n] = jnp.exp2(decay_rows[n] * final[states])
                end_ref[1, n] = final[n]

    return body


def local_scan(
    start_state, step3, drive3, input_map, output_map, decay3, with_output, first, count, into=None
):
    tok_count, rows, lanes = step3.shape
    states = decay3.shape[0]
    blk = 8
    grid_len = count // blk
    lead = first // blk
    smem = pl.BlockSpec(memory_space=pltpu.SMEM)
    seq_spec = pl.BlockSpec((tok_count, blk, lanes), lambda j: (0, j + lead, 0))
    st_spec = pl.BlockSpec((states, blk, lanes), lambda j: (0, j + lead, 0))
    own_seq = pl.BlockSpec((tok_count, blk, lanes), lambda j: (0, j, 0))
    own_st = pl.BlockSpec((states, blk, lanes), lambda j: (0, j, 0))
    if with_output:
        out_shape = [jax.ShapeDtypeStruct((states, count, lanes), jnp.float32)]
        out_specs = [own_st]
    else:
        out_shape = [jax.ShapeDtypeStruct((2, states, count, lanes), jnp.float32)]
        out_specs = [pl.BlockSpec((2, states, blk, lanes), lambda j: (0, 0, j, 0))]
    if with_output:
        out_shape.insert(0, jax.ShapeDtypeStruct((tok_count, rows, lanes), jnp.float32))
        out_specs.insert(0, seq_spec)
    operands = [jnp.concatenate([input_map, output_map], axis=1).reshape(-1), step3, drive3, decay3]
    in_specs = [smem, seq_spec, seq_spec, st_spec]
    aliases = {}
    plain = scan_kernel(with_output)
    extra = 0
    if with_output:
        piece_spec = pl.BlockSpec((2, states, blk, lanes), lambda j: (0, 0, j, 0))
        operands.extend(start_state)
        in_specs.extend([piece_spec] * len(start_state))
        if into is not None:
            aliases = {len(operands): 0}
            operands.append(into)
            in_specs.append(pl.BlockSpec(memory_space=pl.ANY))
            extra = 1
    held = len(start_state) if with_output else 0

    def body(*refs):
        lead_refs = refs[:4]
        pieces = tuple(refs[4 : 4 + held]) if with_output else None
        return plain(*lead_refs, pieces, *refs[4 + held + extra :])

    results = pl.pallas_call(
        body,
        grid=(grid_len,),
        in_specs=in_specs,
        out_specs=out_specs,
        out_shape=out_shape,
        input_output_aliases=aliases,
    )(*operands)
    if with_output:
        return (results[0], results[-1])
    return (None, results[-1])


def per_device(
    tokens,
    norm_gain,
    conv_weight,
    conv_bias,
    proj_weight,
    dt_weight,
    dt_bias,
    decay_rate,
    skip_gain,
    ffn_gain,
    expert_ids,
    route_weights,
    w_gate,
    w_up,
    w_down,
):
    stream = tokens[0].astype(jnp.float32)
    tok_count = stream.shape[0]
    model_width = stream.shape[1]
    kernel = conv_weight.shape[0]
    low_width = dt_weight.shape[0]
    states = decay_rate.shape[0]
    normed = rms_scale(stream, norm_gain).astype(jnp.bfloat16)
    prior_rows = from_behind(normed[tok_count - (kernel - 1) :], "seq", 1)
    padded = jnp.concatenate([prior_rows, normed], axis=0).astype(jnp.float32)
    conv_sum = jnp.zeros((tok_count, model_width), jnp.float32)
    for offset in range(kernel):
        conv_sum = conv_sum + conv_weight[offset] * padded[offset : offset + tok_count]
    conv_out = jax.nn.silu(conv_sum + conv_bias).astype(jnp.bfloat16)
    projected = jnp.dot(conv_out, proj_weight, preferred_element_type=jnp.float32)
    low_rank = projected[:, :low_width].astype(jnp.bfloat16)
    step_size = jax.nn.softplus(
        jnp.dot(low_rank, dt_weight, preferred_element_type=jnp.float32) + dt_bias
    )
    input_map = projected[:, low_width : low_width + states]
    output_map = projected[:, low_width + states :]
    decay_neg = -decay_rate
    conv_float = conv_out.astype(jnp.float32)
    lanes = 128
    rows = model_width // lanes
    chunks = 2
    count = rows // chunks
    step3 = step_size.reshape(tok_count, rows, lanes)
    drive3 = conv_out.reshape(tok_count, rows, lanes)
    decay3 = (decay_neg * math.log2(math.e)).reshape(states, rows, lanes)
    zero_state = jnp.zeros((states, count, lanes), jnp.float32)
    peers = lax.axis_size("seq")
    inflow = []
    for c in range(chunks):
        _, end_state = local_scan(
            None, step3, drive3, input_map, output_map, decay3, False, c * count, count
        )
        summary = end_state
        inflow.append([from_behind(summary, "seq", k) for k in range(peers - 1, 0, -1)])
    scanned3 = None
    for c in range(chunks):
        incoming = inflow[c]
        scanned3, _ = local_scan(
            incoming, step3, drive3, input_map, output_map, decay3, True, c * count, count, scanned3
        )
    scanned = scanned3.reshape(tok_count, model_width)
    hidden_state = stream + (scanned + skip_gain * conv_float)
    ffn_in = rms_scale(hidden_state, ffn_gain).astype(jnp.bfloat16)
    owners = lax.axis_size("expert")
    experts = owners * w_gate.shape[0]
    capacity = 4 * tok_count // owners
    chosen = expert_ids[0].reshape(-1)
    onehot = (chosen[:, None] == jnp.arange(experts, dtype=jnp.int32)[None, :]).astype(jnp.bfloat16)
    pair_ids = jnp.arange(chosen.shape[0], dtype=jnp.int32)
    earlier = (pair_ids[:, None] > pair_ids[None, :]).astype(jnp.bfloat16)
    before = jnp.dot(earlier, onehot, preferred_element_type=jnp.float32)
    slot_pos = jnp.sum(before * onehot.astype(jnp.float32), axis=1).astype(jnp.int32)
    dest_row = chosen * capacity + slot_pos
    slot_ids = jnp.arange(experts * capacity, dtype=jnp.int32)
    pair_rows = dest_row.reshape(tok_count, 2)
    place_map = (
        (slot_ids[:, None] == pair_rows[None, :, 0]) | (slot_ids[:, None] == pair_rows[None, :, 1])
    ).astype(jnp.bfloat16)
    outgoing = jnp.dot(place_map, ffn_in, preferred_element_type=jnp.float32).astype(jnp.bfloat16)
    outgoing = outgoing.reshape(experts, capacity, model_width)
    received = lax.all_to_all(outgoing, "expert", split_axis=0, concat_axis=0, tiled=True)
    recv_shape = received.shape
    rows_in = received.reshape(-1, model_width)
    gate_part = jnp.dot(rows_in, w_gate[0], preferred_element_type=jnp.float32)
    up_part = jnp.dot(rows_in, w_up[0], preferred_element_type=jnp.float32)
    inner_act = (jax.nn.silu(gate_part) * up_part).astype(jnp.bfloat16)
    result = jnp.dot(inner_act, w_down[0], preferred_element_type=jnp.float32).astype(jnp.bfloat16)
    returned = lax.all_to_all(
        result.reshape(recv_shape), "expert", split_axis=0, concat_axis=0, tiled=True
    )
    flat_back = returned.reshape(experts * capacity, model_width)
    picks = [
        jnp.dot(
            (pair_rows[:, k][:, None] == slot_ids[None, :]).astype(jnp.bfloat16),
            flat_back,
            preferred_element_type=jnp.bfloat16,
        ).astype(jnp.float32)
        for k in range(2)
    ]
    route_scale = route_weights[0]
    routed = route_scale[:, 0:1] * picks[0] + route_scale[:, 1:2] * picks[1]
    block_out = (hidden_state + routed).astype(jnp.bfloat16)
    return block_out[None]


def solution(mesh):
    in_specs = (
        P("expert", "seq", None),
        P(),
        P(),
        P(),
        P(),
        P(),
        P(),
        P(),
        P(),
        P(),
        P("expert", "seq", None),
        P("expert", "seq", None),
        P("expert", None, None),
        P("expert", None, None),
        P("expert", None, None),
    )
    out_specs = P("expert", "seq", None)
    return jax.shard_map(
        per_device, mesh=mesh, in_specs=in_specs, out_specs=out_specs, check_vma=False
    )
```
